256 devices in a mesh: seq: 64 (over y, z, core), ffn: 4 (over x).
Axes of the slice: x: 4, y: 4, z: 8, core: 2. Of those that a mesh axis runs over, the one named last changes fastest.
Arguments:
- child_feat: bfloat16 [32768, 1024], P('seq'), may hold values from -6 to 6
- parent_feat: bfloat16 [4096, 1024], P('seq'), may hold values from -6 to 6
- child_parent: int32 [32768], P('seq'), may hold values from 0 to 63
- owner: int32 [32768, 1], P('seq'), may hold values from 0 to 63; in each aligned block of 512 rows (0 to 511, 512 to 1023, ...) at most 16 rows name the same one
- log_gate: float32 [16, 65536], P('ffn', 'seq'), may hold values from -1 to 0
- norm_gain: bfloat16 [1024], replicated, may hold values from 0.3984375 to 1.59375
- w_query: bfloat16 [1024, 1024], P(None, 'ffn'), may hold values from -0.1875 to 0.1875
- w_key: bfloat16 [1024, 1024], P(None, 'ffn'), may hold values from -0.1875 to 0.1875
- w_value: bfloat16 [1024, 1024], P(None, 'ffn'), may hold values from -0.1875 to 0.1875
- head_gain: bfloat16 [1024], P('ffn'), may hold values from 0.25 to 1.75
- w_out: bfloat16 [1024, 1024], P('ffn'), may hold values from -0.1875 to 0.1875
- ffn_gain: bfloat16 [1024], replicated, may hold values from 0.3984375 to 1.59375
- w_up: bfloat16 [1024, 4096], P(None, 'ffn'), may hold values from -0.1875 to 0.1875
- w_down: bfloat16 [4096, 1024], P('ffn'), may hold values from -0.09375 to 0.09375
Outputs:
- child_out: bfloat16 [32768, 1024], P('seq', 'ffn')
The draws below stay inside these ranges and needn't reach their ends.
Inputs may be any that keep to these rules, and one draw needn't show every extreme that they name: The parent of child i is row (i // 512) * 64 + child_parent[i] of parent_feat. Among the 512 children of one index of seq, at most 16 name the same owner, and in every draw some owner is named exactly 16 times by some block.
All inputs are finite; a program needn't handle non-finite values.
Results may differ from the reference program's by a relative error of at most 0.013.
Values may be sent and summed in bfloat16 or wider, within the bound.
A program may use at most 64 MiB of HBM per device.

```python
import math
import jax
import jax.numpy as jnp
import numpy as np
from jax import lax

D = 1024
HEAD_TOTAL = 16
HD = 64
FF = 4096
TOK_DEV = 512
PAR_DEV = 64
CAP = 16
SLOT_DEV = 1024
TOKENS = 32768
PARENTS = 4096
SLOT_TOTAL = 65536
N_SEQ = 64
N_FFN = 4


def draw_log_gate(key, part):
    random_subkeys = jax.random.split(key, 7)
    fast_share = 0.5
    forgetful = jax.random.uniform(random_subkeys[0], (HEAD_TOTAL,)) < fast_share
    fast_rate = 1.0 / jax.random.uniform(random_subkeys[1], (HEAD_TOTAL,), minval=30.0, maxval=50.0)
    slow_rate = math.log(10.0) * jax.random.uniform(random_subkeys[2], (HEAD_TOTAL,), minval=0.05, maxval=0.15) / SLOT_TOTAL
    retain_rate = jnp.where(forgetful, fast_rate, slow_rate)
    block_count = SLOT_TOTAL // SLOT_DEV
    per_block = jnp.exp(jax.random.uniform(random_subkeys[3], (HEAD_TOTAL, block_count), minval=-math.log(2.0), maxval=math.log(2.0)))
    spread_out = jnp.repeat(per_block, SLOT_DEV, axis=1)
    roughness = jnp.exp(jax.random.uniform(random_subkeys[4], (HEAD_TOTAL, SLOT_TOTAL), minval=-math.log(2.0), maxval=math.log(2.0)))
    gate_logarithms = -retain_rate[:, None] * spread_out * roughness
    surge_position = jax.random.randint(random_subkeys[5], (HEAD_TOTAL, 3), 0, SLOT_TOTAL)
    surge_penalty = jnp.log(jax.random.uniform(random_subkeys[6], (HEAD_TOTAL, 3), minval=0.55, maxval=0.75))
    slot_numbers = jnp.arange(SLOT_TOTAL, dtype=jnp.int32)
    surge_flags = slot_numbers[None, None, :] == surge_position[:, :, None]
    gate_logarithms = gate_logarithms + jnp.sum(jnp.where(surge_flags, surge_penalty[:, :, None], 0.0), axis=1)
    return jnp.maximum(gate_logarithms, -1.0).astype(jnp.float32)


def plant(values, rng, smallest, largest):
    longest = values.shape.index(max(values.shape))
    spots = []
    for shift in (0, 1):
        where = [jax.random.randint(jax.random.fold_in(rng, axis), (), 0, length) for axis, length in enumerate(values.shape)]
        where[longest] = (where[longest] + shift) % values.shape[longest]
        spots.append(tuple(where))
    return values.at[spots[0]].set(smallest).at[spots[1]].set(largest)


def steps_of(own_key, extent, cuts, low, high):
    factor_of, own = 1.0, jax.random.fold_in(own_key, 6)
    for axis_at, shards_of in cuts:
        steps = jnp.exp(jax.random.uniform(jax.random.fold_in(own, axis_at), (shards_of,), jnp.float32, low / len(cuts), high / len(cuts)))
        factor_of = factor_of * jnp.repeat(steps, extent[axis_at] // shards_of).reshape([-1 if axis == axis_at else 1 for axis in range(len(extent))])
    return factor_of


def routed_block(stream_key, own, number, rows, count, top, limit, slope):
    order = jax.random.permutation(stream_key, count)
    packed, usual = shares(count, rows * top, limit, slope, True), shares(count, rows * top, limit, slope, False)
    places = jnp.arange(count)

    def named(lengths, offset_by):
        used = int((lengths > 0).sum())
        fixed = max(1, used // 4)
        shifted = fixed + (places - fixed + offset_by * (used - fixed)) % max(1, count - fixed)
        return jnp.zeros((count,), jnp.int32).at[order[jnp.where(places < fixed, places, shifted)]].set(jnp.asarray(lengths, jnp.int32))

    lengths = jnp.where(number % 4 == 0, named(packed, number // 4), named(usual, number - number // 4 - 1))
    mixed = jax.random.permutation(jax.random.fold_in(own, 3), count)
    source_of, taker = mixed[0:count // 2 * 2:2], mixed[1:count // 2 * 2:2]
    slack = jnp.minimum(lengths[source_of] - 1, limit - lengths[taker]) // 2
    slack = jnp.where((source_of == order[0]) | (taker == order[0]) | (lengths[taker] == 0), 0, jnp.maximum(slack, 0))
    shifted = jax.random.randint(jax.random.fold_in(own, 4), (count // 2,), 0, 1 << 20) % (slack + 1)
    lengths = lengths.at[source_of].add(-shifted).at[taker].add(shifted)
    items = jnp.searchsorted(jnp.cumsum(lengths), jnp.arange(rows * top), side="right").astype(jnp.int32)
    grid = items.reshape(top, rows).T
    grid = grid[jax.random.permutation(jax.random.fold_in(own, 1), rows)]
    offset_by = jax.random.randint(jax.random.fold_in(own, 2), (rows, 1), 0, top)
    return jnp.take_along_axis(grid, (jnp.arange(top)[None, :] + offset_by) % top, axis=1)


def shares(amount, total, limit, lean, full):
    portions = [(1 << 20) // math.isqrt(rank ** lean) + 1 for rank in range(1, amount + 1)]
    largest = limit if full else min(limit, max(-(-total // amount), total * portions[0] // sum(portions)))
    least = 1 if total - largest >= amount - 1 else 0
    counts, surplus = [largest] + [least] * (amount - 1), total - largest - least * (amount - 1)
    while surplus > 0:
        free = [i for i in range(1, amount) if counts[i] < largest] or [i for i in range(1, amount) if counts[i] < limit]
        mass, left = sum([portions[i] for i in free]), surplus
        for i in free:
            more = min(limit - counts[i], max(1, left * portions[i] // mass), surplus)
            counts[i] = counts[i] + more
            surplus = surplus - more
    return np.array(counts)


def normal_values(own_key, shape, width, reach, shards=(), kind=jnp.bfloat16):
    array = width * jax.random.normal(own_key, shape, jnp.float32)
    if shards:
        array = array * steps_of(own_key, shape, shards, -0.22, 0.18)
    return jnp.clip(array, -reach, reach).astype(kind)


def setup_inputs(seed: int = 0) -> dict:
    arg_keys = jax.random.split(jax.random.key(seed), 15)
    child_feat = normal_values(arg_keys[0], (TOKENS, D), 1.0, 6.0, ((0, 64),))
    parent_feat = normal_values(arg_keys[1], (PARENTS, D), 0.7, 6.0, ((0, 64),))
    child_parent = plant(jax.random.randint(arg_keys[2], (TOKENS,), 0, PAR_DEV), jax.random.fold_in(arg_keys[2], 1), 0, PAR_DEV - 1).astype(jnp.int32)
    owner_keys = jax.random.split(jax.random.fold_in(arg_keys[3], 1), TOKENS // TOK_DEV)
    owner_turns = jax.random.permutation(jax.random.fold_in(arg_keys[3], 3), TOKENS // TOK_DEV)
    owner = jax.vmap(lambda own, number: routed_block(jax.random.fold_in(arg_keys[3], 2), own, number, TOK_DEV, N_SEQ, 1, CAP, 1))(owner_keys, owner_turns).reshape((TOKENS, 1))
    log_gate = draw_log_gate(jax.random.fold_in(arg_keys[14], 71), 0)
    norm_gain = jnp.clip(1.0 + 0.12 * jax.random.normal(arg_keys[5], (D,), jnp.float32), 0.3984375, 1.59375).astype(jnp.bfloat16)
    w_query = normal_values(arg_keys[6], (D, HEAD_TOTAL * HD), D ** -0.5, 0.1875, ((1, 4),))
    w_key = normal_values(arg_keys[7], (D, HEAD_TOTAL * HD), D ** -0.5, 0.1875, ((1, 4),))
    w_value = normal_values(arg_keys[8], (D, HEAD_TOTAL * HD), D ** -0.5, 0.1875, ((1, 4),))
    head_gain = jnp.clip(1.0 + 0.15 * jax.random.normal(arg_keys[9], (HEAD_TOTAL * HD,), jnp.float32), 0.25, 1.75).astype(jnp.bfloat16)
    w_out = normal_values(arg_keys[10], (HEAD_TOTAL * HD, D), (HEAD_TOTAL * HD) ** -0.5, 0.1875, ((0, 4),))
    ffn_gain = jnp.clip(1.0 + 0.12 * jax.random.normal(arg_keys[11], (D,), jnp.float32), 0.3984375, 1.59375).astype(jnp.bfloat16)
    w_up = normal_values(arg_keys[12], (D, FF), D ** -0.5, 0.1875, ((1, 4),))
    w_down = normal_values(arg_keys[13], (FF, D), FF ** -0.5, 0.09375, ((0, 4),))
    return dict(child_feat=child_feat, parent_feat=parent_feat, child_parent=child_parent, owner=owner, log_gate=log_gate, norm_gain=norm_gain, w_query=w_query, w_key=w_key, w_value=w_value, head_gain=head_gain, w_out=w_out, ffn_gain=ffn_gain, w_up=w_up, w_down=w_down)


EPSILON = 1e-05
PRECISE = lax.Precision.HIGHEST

def rounded(values):
    return lax.optimization_barrier(values.astype(jnp.bfloat16)).astype(jnp.float32)

def row_norm(values, scales):
    return values * lax.rsqrt(lax.optimization_barrier(jnp.mean(values * values, axis=-1, keepdims=True)) + EPSILON) * scales

def quarter_sum(lhs_rows, rhs_cols):
    column_span = lhs_rows.shape[1] // N_FFN
    running_sum = jnp.zeros((lhs_rows.shape[0], rhs_cols.shape[1]), jnp.float32)
    for quarter in range(N_FFN):
        partial_term = jnp.dot(lhs_rows[:, quarter * column_span:(quarter + 1) * column_span], rhs_cols[quarter * column_span:(quarter + 1) * column_span], preferred_element_type=jnp.float32)
        running_sum = running_sum + rounded(partial_term)
    return running_sum

def slot_positions(owner_ids):
    grouped = owner_ids.reshape(N_SEQ, TOK_DEV)
    matched = (grouped[:, :, None] == jnp.arange(N_SEQ, dtype=jnp.int32)[None, None, :]).astype(jnp.int32)
    within = lax.optimization_barrier(jnp.sum(matched * (jnp.cumsum(matched, axis=1) - 1), axis=2))
    sources = jnp.arange(N_SEQ, dtype=jnp.int32)[:, None]
    return (grouped * SLOT_DEV + sources * CAP + within).reshape(TOKENS).astype(jnp.int32)

def reference(child_feat, parent_feat, child_parent, owner, log_gate, norm_gain, w_query, w_key, w_value, head_gain, w_out, ffn_gain, w_up, w_down):
    parent_rows = jnp.arange(TOKENS, dtype=jnp.int32) // TOK_DEV * PAR_DEV + child_parent
    joined = (child_feat.astype(jnp.float32) + parent_feat.astype(jnp.float32)[parent_rows]).astype(jnp.bfloat16)
    slot_of = slot_positions(owner[:, 0])
    slots = jnp.zeros((SLOT_TOTAL, D), jnp.bfloat16).at[slot_of].set(joined)
    slot_blocks = slots.reshape(N_SEQ, SLOT_DEV, D)
    gate_blocks = log_gate.reshape(HEAD_TOTAL, N_SEQ, SLOT_DEV).transpose(1, 0, 2)
    head_scales = head_gain.astype(jnp.float32).reshape(HEAD_TOTAL, HD)

    def advance(carried, block_item):
        slot_rows, gate_logarithms = block_item
        span_rows = slot_rows.shape[0]
        residual_in = slot_rows.astype(jnp.float32)
        normed = row_norm(residual_in, norm_gain.astype(jnp.float32)).astype(jnp.bfloat16)
        queries = rounded(jnp.dot(normed, w_query, preferred_element_type=jnp.float32)).reshape(span_rows, HEAD_TOTAL, HD)
        key_rows = rounded(jnp.dot(normed, w_key, preferred_element_type=jnp.float32)).reshape(span_rows, HEAD_TOTAL, HD)
        value_rows = rounded(jnp.dot(normed, w_value, preferred_element_type=jnp.float32)).reshape(span_rows, HEAD_TOTAL, HD)
        running = jnp.cumsum(gate_logarithms, axis=1)
        position = jnp.arange(span_rows, dtype=jnp.int32)
        causal = (position[:, None] >= position[None, :])[None]
        spacing = running[:, :, None] - running[:, None, :]
        decay_mat = jnp.where(causal, jnp.exp(jnp.where(causal, spacing, 0.0)), 0.0)
        scores = jnp.einsum('shd,thd->hst', queries, key_rows)
        mixing = rounded(scores * decay_mat)
        inside = jnp.einsum('hst,thd->shd', mixing, value_rows)
        outside = jnp.exp(running).T[:, :, None] * jnp.einsum('shd,hde->she', queries, carried, precision=PRECISE)
        combined = inside + outside
        per_head = combined * lax.rsqrt(lax.optimization_barrier(jnp.mean(combined * combined, axis=-1, keepdims=True)) + EPSILON) * head_scales[None]
        flattened = per_head.astype(jnp.bfloat16).reshape(span_rows, HEAD_TOTAL * HD)
        hidden = residual_in + quarter_sum(flattened, w_out)
        second = row_norm(hidden, ffn_gain.astype(jnp.float32)).astype(jnp.bfloat16)
        expanded = jax.nn.gelu(jnp.dot(second, w_up, preferred_element_type=jnp.float32)).astype(jnp.bfloat16)
        refined = (hidden + quarter_sum(expanded, w_down)).astype(jnp.bfloat16)
        block_end = running[:, -1]
        fading = jnp.exp(block_end[:, None] - running).T
        new_state = jnp.exp(block_end)[:, None, None] * carried + jnp.einsum('shd,she->hde', key_rows * fading[:, :, None], value_rows, precision=PRECISE)
        return (new_state, refined)
    initial = jnp.zeros((HEAD_TOTAL, HD, HD), jnp.float32)
    _, outputs = lax.scan(advance, initial, (slot_blocks, gate_blocks))
    return outputs.reshape(SLOT_TOTAL, D)[slot_of]
```

```python
import jax
import jax.numpy as jnp
from jax import lax
from jax.experimental import pallas as pl
from jax.experimental.pallas import tpu as pltpu
from jax.sharding import PartitionSpec as P

D = 1024
HD = 64
HEADS = 4
Q = 256
TOK = 512
PAR = 64
SLOT = 1024
N = 64
CAP = 16
GRP = 16
CH = 256
ROWS = 128
HALF = 64
EPS = 1e-05
F32 = jnp.float32
BF16 = jnp.bfloat16
MESH = pl.DeviceIdType.MESH
EXACT = lax.Precision.HIGHEST
REL = (0, 1, 3, 2)


def nt(a, b, precision=None):
    return lax.dot_general(
        a, b, (((1,), (1,)), ((), ())), precision=precision, preferred_element_type=F32
    )


def tn(a, b):
    return lax.dot_general(a, b, (((0,), (0,)), ((), ())), preferred_element_type=F32)


def nn(a, b, precision=None):
    return jnp.dot(a, b, precision=precision, preferred_element_type=F32)


def iota(shape, dim):
    return lax.broadcasted_iota(jnp.int32, shape, dim)


def kernel(
    child, parent, cp_row, own_row, gate, ngain, wq, wk, wv, hgain, wo, fgain, wu, wd,
    out,
    child_v, parent_v, wqkv, wo_v, wu_v, wd_v,
    joined, pick_t, outgoing, slots, normed, qkv, att, ccol, crow, loc, offs,
    s_send, s_recv, p_send, p_recv, heads_out, back,
    part, via, comb, fin, hid, hb,
    in_sem, a_send, a_recv, g_send, g_recv, st_send, st_recv, pf_send, pf_recv, b_send, b_recv,
    v_send, v_recv, f_send, f_recv, h_send, h_recv,
):
    me = lax.axis_index("seq")
    fx = lax.axis_index("ffn")
    my_y = me // GRP
    my_zc = me % GRP
    left, right, far = (fx + 3) % 4, (fx + 1) % 4, (fx + 2) % 4

    cols = pl.ds(pl.multiple_of(fx * Q, Q), Q)
    loads = [
        (child.at[:, cols], child_v),
        (parent.at[:, cols], parent_v),
        (wq, wqkv.at[:, pl.ds(0, Q)]),
        (wk, wqkv.at[:, pl.ds(Q, Q)]),
        (wv, wqkv.at[:, pl.ds(2 * Q, Q)]),
        (wo, wo_v),
        (wu, wu_v),
        (wd, wd_v),
    ]
    loads = [pltpu.make_async_copy(s, d, in_sem.at[i]) for i, (s, d) in enumerate(loads)]
    for copy in loads:
        copy.start()

    barrier = pltpu.get_barrier_semaphore()

    def greet(k, _):
        pl.semaphore_signal(
            barrier, inc=1, device_id=((me + k) % N, fx), device_id_type=MESH
        )
        return 0

    lax.fori_loop(1, N, greet, 0)
    for k in (1, 2, 3):
        pl.semaphore_signal(barrier, inc=1, device_id=(me, (fx + k) % 4), device_id_type=MESH)

    owners = own_row[...]
    member = iota((N, TOK), 0) == owners
    matched = member.astype(F32)
    upper = (iota((TOK, TOK), 0) <= iota((TOK, TOK), 1)).astype(F32).astype(BF16)
    counts = nn(matched.astype(BF16), upper)
    within = jnp.sum(matched * (counts - 1.0), axis=0, keepdims=True)
    target = owners.astype(F32) * float(CAP) + within
    eye = (iota((TOK, TOK), 0) == iota((TOK, TOK), 1)).astype(F32)
    target_col = nt(eye, jnp.broadcast_to(target, (8, TOK)), EXACT)[:, 0:1]
    pick_t[...] = (
        (iota((TOK, SLOT), 1) == (target_col + 0.5).astype(jnp.int32)).astype(F32).astype(BF16)
    )
    parents = (iota((PAR, TOK), 0) == cp_row[...]).astype(F32).astype(BF16)
    loads[0].wait()
    loads[1].wait()
    joined[...] = (child_v[...].astype(F32) + tn(parents, parent_v[...])).astype(BF16)
    target_int = (target + 0.5).astype(jnp.int32)
    for i in range(4):
        pick = (iota((CH, TOK), 0) + i * CH == target_int).astype(F32).astype(BF16)
        outgoing[pl.ds(i * GRP, GRP)] = (
            nn(pick, joined[...]).astype(BF16).reshape(GRP, CAP, Q)
        )

    pl.semaphore_wait(barrier, N - 1 + 3)

    def slot_copy(dest, rel):
        return pltpu.make_async_remote_copy(
            src_ref=outgoing.at[dest],
            dst_ref=slots.at[fx, me],
            send_sem=a_send,
            recv_sem=a_recv.at[(4 - rel) % 4],
            device_id=(dest, fx),
            device_id_type=MESH,
        )

    own_slots = pltpu.make_async_copy(outgoing.at[me], slots.at[fx, me], a_recv.at[0])
    own_slots.start()
    for rel in REL:
        base = (my_y + rel) % 4 * GRP

        def send(j, _, base=base, rel=rel):
            half = (j + 1) // 2
            off = half * (j % 2) + (GRP - half) * (1 - j % 2)
            slot_copy(base + (my_zc + off) % GRP, rel).start()
            return 0

        lax.fori_loop(1 if rel == 0 else 0, GRP, send, 0)

    causal = iota((CH, CH), 0) >= iota((CH, CH), 1)
    tri = causal.astype(F32)
    lane_head = iota((1, Q), 1) // HD

    def spread(columns):
        wide = jnp.zeros((columns.shape[0], Q), F32)
        for h in range(HEADS):
            wide = jnp.where(lane_head == h, columns[:, h : h + 1], wide)
        return wide

    block_end = jnp.zeros((1, HEADS), F32)
    for y in range(4):
        g = gate[:, pl.ds(y * CH, CH)]
        crow[y] = nt(g, tri, EXACT)
        columns = nt(tri, g, EXACT)
        ccol[y] = columns
        offs[y] = spread(block_end)
        block_end = block_end + columns[CH - 1 : CH, :]

    def ring(src, dst, send_sem, recv_sem, to):
        return pltpu.make_async_remote_copy(
            src_ref=src, dst_ref=dst, send_sem=send_sem, recv_sem=recv_sem,
            device_id=(me, to), device_id_type=MESH,
        )

    def gather_first(rel):
        rows = pl.ds((my_y + rel) % 4 * GRP, GRP)
        mine = slots.at[fx, rows]
        return [
            ring(mine, mine, g_send.at[rel, 0], g_recv.at[rel, 0], right),
            ring(mine, mine, g_send.at[rel, 1], g_recv.at[rel, 1], left),
        ]

    def gather_second(rel):
        start = (my_y + rel) % 4 * GRP
        a = slots.at[left, pl.ds(start, GRP // 2)]
        b = slots.at[right, pl.ds(start + GRP // 2, GRP // 2)]
        return [
            ring(a, a, g_send.at[rel, 2], g_recv.at[rel, 2], right),
            ring(b, b, g_send.at[rel, 3], g_recv.at[rel, 3], left),
        ]

    def slots_in(rel):
        here = slots.at[fx, pl.ds((my_y + rel) % 4 * GRP, GRP)]
        pltpu.make_async_copy(here, here, a_recv.at[rel]).wait()
        for copy in gather_first(rel):
            copy.start()

    def slots_on(rel):
        for copy, after in zip(gather_first(rel), gather_second(rel)):
            copy.wait_recv()
            after.start()

    def project(rel):
        y = (my_y + rel) % 4
        for copy in gather_second(rel):
            copy.wait_recv()
        squares = jnp.zeros((CH, 1), F32)
        for q in range(4):
            x = slots[q, pl.ds(y * GRP, GRP)].reshape(CH, Q).astype(F32)
            squares = squares + jnp.sum(x * x, axis=1, keepdims=True)
        scale = lax.rsqrt(squares / D + EPS)
        for q in range(4):
            x = slots[q, pl.ds(y * GRP, GRP)].reshape(CH, Q).astype(F32)
            gain = ngain[:, pl.ds(q * Q, Q)].astype(F32)
            normed[:, pl.ds(q * Q, Q)] = (x * scale * gain).astype(BF16)
        qkv[y] = nn(normed[...], wqkv[...]).astype(BF16)

    order = list(REL)
    for i in range(6):
        if i < 4:
            slots_in(order[i])
        if 1 <= i < 5:
            slots_on(order[i - 1])
        if i == 1:
            for copy in loads[2:5]:
                copy.wait()
        if i >= 2:
            project(order[i - 2])

    same_head = iota((Q, Q), 0) // HD == iota((Q, Q), 1) // HD
    carried = jnp.zeros((Q, Q), F32)
    for y in range(4):
        loc[y] = carried
        ends = ccol[y, pl.ds(CH - 1, 1), :]
        fade = jnp.exp(spread(ends - ccol[y]))
        added = tn(
            (qkv[y, :, pl.ds(Q, Q)].astype(F32) * fade).astype(BF16),
            qkv[y, :, pl.ds(2 * Q, Q)],
        )
        carried = jnp.exp(spread(ends)) * carried + jnp.where(same_head, added, 0.0)
    state = jnp.zeros((HD, Q), F32)
    for h in range(HEADS):
        state = state + carried[h * HD : (h + 1) * HD, :]
    lane = iota((1, 128), 1)
    ends = jnp.zeros((1, 128), F32)
    for h in range(HEADS):
        ends = jnp.where(lane == h, block_end[:, h : h + 1], ends)
    s_send[:, 0, :] = jnp.concatenate([state, jnp.broadcast_to(ends, (HD, 128))], axis=1)

    def to_all(src, dst, send_sem, recv_sem):
        pltpu.make_async_copy(src.at[me], dst.at[me], recv_sem).start()

        def send(k, _):
            dest = (me + k) % N
            pltpu.make_async_remote_copy(
                src_ref=src.at[dest], dst_ref=dst.at[me], send_sem=send_sem, recv_sem=recv_sem,
                device_id=(dest, fx), device_id_type=MESH,
            ).start()
            return 0

        lax.fori_loop(1, N, send, 0)

    def arrived(ref, sem):
        pltpu.make_async_copy(ref, ref, sem).wait()

    to_all(s_send, s_recv, st_send, st_recv)

    def inside(y):
        q = qkv[y, :, pl.ds(0, Q)]
        k = qkv[y, :, pl.ds(Q, Q)]
        v = qkv[y, :, pl.ds(2 * Q, Q)]
        total = jnp.zeros((CH, Q), F32)
        for h in range(HEADS):
            mine = (lane_head == h).astype(F32).astype(BF16)
            scores = nt(q * mine, k)
            spacing = ccol[y, :, pl.ds(h, 1)] - crow[y, pl.ds(h, 1), :]
            decay = jnp.where(causal, jnp.exp(jnp.minimum(spacing, 0.0)), 0.0)
            total = total + nn((scores * decay).astype(BF16), v * mine)
        att[y] = total

    inside(0)
    inside(1)
    arrived(s_recv, st_recv)
    got = s_recv[:, 0, :]
    got_ends = got[:, Q:]
    states = got[:, :Q]
    tri_n = (iota((N, N), 0) >= iota((N, N), 1)).astype(F32)
    upto = nn(tri_n, got_ends, EXACT)
    before = upto - got_ends
    upto_t = upto.T
    earlier = iota((N, N), 0) > iota((N, N), 1)
    prefix = jnp.zeros((N, Q), F32)
    for h in range(HEADS):
        spacing = before[:, h : h + 1] - upto_t[h : h + 1, :]
        weight = jnp.where(earlier, jnp.exp(jnp.minimum(spacing, 0.0)), 0.0)
        prefix = jnp.where(lane_head == h, nn(weight, states, EXACT), prefix)
    p_send[:, 0, :] = prefix
    to_all(p_send, p_recv, pf_send, pf_recv)
    inside(2)
    inside(3)
    arrived(p_recv, pf_recv)
    incoming = p_recv[:, 0, :]
    incoming = jnp.where(same_head, jnp.concatenate([incoming] * HEADS, axis=0), 0.0)

    ones_head = same_head.astype(F32).astype(BF16)
    for rel in REL:
        y = (my_y + rel) % 4
        at_start = jnp.exp(offs[y]) * incoming + loc[y]
        outside = nn(qkv[y, :, pl.ds(0, Q)], at_start.astype(BF16))
        o = att[y] + jnp.exp(spread(ccol[y])) * outside
        squares = o * o
        high = squares.astype(BF16)
        low = (squares - high.astype(F32)).astype(BF16)
        mean = (nn(high, ones_head) + nn(low, ones_head)) / HD
        o = o * lax.rsqrt(mean + EPS) * hgain[...].astype(F32)
        heads_out[pl.ds(y * GRP, GRP)] = o.astype(BF16).reshape(GRP, CAP, Q)
        if rel == 0:
            pltpu.make_async_copy(heads_out.at[me], back.at[me], b_recv).start()

        def send(j, _, y=y):
            half = (j + 1) // 2
            off = half * (j % 2) + (GRP - half) * (1 - j % 2)
            dest = y * GRP + (my_zc + off) % GRP
            pltpu.make_async_remote_copy(
                src_ref=heads_out.at[dest], dst_ref=back.at[me], send_sem=b_send, recv_sem=b_recv,
                device_id=(dest, fx), device_id_type=MESH,
            ).start()
            return 0

        lax.fori_loop(1 if rel == 0 else 0, GRP, send, 0)

    top, bottom = pl.ds(0, HALF), pl.ds(HALF, HALF)

    def scatter_first(s, c):
        return [
            ring(part.at[s, c, far, top], via.at[s, c, 0], v_send.at[s, c, 0], v_recv.at[s, c, 0], right),
            ring(part.at[s, c, far, bottom], via.at[s, c, 1], v_send.at[s, c, 1], v_recv.at[s, c, 1], left),
        ]

    def scatter_own(s, c):
        return [
            ring(part.at[s, c, right, bottom], fin.at[s, c, 0, 1], f_send.at[s, c, 0, 1], f_recv.at[s, c, 0, 1], right),
            ring(part.at[s, c, left, top], fin.at[s, c, 1, 0], f_send.at[s, c, 1, 0], f_recv.at[s, c, 1, 0], left),
        ]

    def scatter_joint(s, c):
        return [
            ring(comb.at[s, c, 0], fin.at[s, c, 0, 0], f_send.at[s, c, 0, 0], f_recv.at[s, c, 0, 0], right),
            ring(comb.at[s, c, 1], fin.at[s, c, 1, 1], f_send.at[s, c, 1, 1], f_recv.at[s, c, 1, 1], left),
        ]

    def scatter_start(s, c, product):
        for q in range(4):
            part[s, c, q] = product[:, q * Q : (q + 1) * Q].astype(BF16)
        for copy in scatter_first(s, c) + scatter_own(s, c):
            copy.start()

    def scatter_on(s, c):
        pieces = [(right, top), (left, bottom)]
        for d, (copy, after) in enumerate(zip(scatter_first(s, c), scatter_joint(s, c))):
            copy.wait_recv()
            whose, rows = pieces[d]
            comb[s, c, d] = (
                part[s, c, whose, rows, :].astype(F32) + via[s, c, d].astype(F32)
            ).astype(BF16)
            after.start()

    def scattered(s, c):
        for copy in scatter_own(s, c) + scatter_joint(s, c):
            copy.wait_recv()
        total = part[s, c, fx].astype(F32)
        for d in range(2):
            total = total + fin[s, c, d].reshape(ROWS, Q).astype(F32)
        return total

    def hidden_first(c):
        mine = hb.at[fx, c]
        return [
            ring(mine, mine, h_send.at[c, 0], h_recv.at[c, 0], right),
            ring(mine, mine, h_send.at[c, 1], h_recv.at[c, 1], left),
        ]

    def hidden_second(c):
        a, b = hb.at[left, c, top], hb.at[right, c, bottom]
        return [
            ring(a, a, h_send.at[c, 2], h_recv.at[c, 2], right),
            ring(b, b, h_send.at[c, 3], h_recv.at[c, 3], left),
        ]

    def hidden_start(c):
        rows = pl.ds(c * ROWS, ROWS)
        value = joined[rows, :].astype(F32) + scattered(0, c)
        hid[c] = value
        hb[fx, c] = value.astype(BF16)
        for copy in hidden_first(c):
            copy.start()

    def hidden_on(c):
        for copy, after in zip(hidden_first(c), hidden_second(c)):
            copy.wait_recv()
            after.start()

    def feed_forward(c):
        for copy in hidden_second(c):
            copy.wait_recv()
        squares = jnp.zeros((ROWS, 1), F32)
        scaled = []
        for q in range(4):
            x = hb[q, c].astype(F32)
            squares = squares + jnp.sum(x * x, axis=1, keepdims=True)
            scaled.append((x * fgain[:, pl.ds(q * Q, Q)].astype(F32)).astype(BF16))
        u = nn(jnp.concatenate(scaled, axis=1), wu_v[...]) * lax.rsqrt(squares / D + EPS)
        expanded = jax.nn.gelu(u).astype(BF16)
        scatter_start(1, c, nn(expanded, wd_v[...]))

    def finish(c):
        out[pl.ds(c * ROWS, ROWS), :] = (hid[c] + scattered(1, c)).astype(BF16)

    for copy in loads[5:]:
        copy.wait()
    arrived(back, b_recv)
    for c in range(4):
        rows = pl.ds(c * ROWS, ROWS)
        heads = nn(pick_t[rows, :], back[...].reshape(SLOT, Q)).astype(BF16)
        scatter_start(0, c, nn(heads, wo_v[...]))
    steps = [
        (0, lambda c: scatter_on(0, c)),
        (1, hidden_start),
        (2, hidden_on),
        (3, feed_forward),
        (5, lambda c: scatter_on(1, c)),
        (6, finish),
    ]
    for i in range(10):
        for delay, step in steps:
            if 0 <= i - delay < 4:
                step(i - delay)

    arrived(outgoing.at[pl.ds(0, N - 1)], a_send)
    arrived(s_send.at[pl.ds(0, N - 1)], st_send)
    arrived(p_send.at[pl.ds(0, N - 1)], pf_send)
    arrived(heads_out.at[pl.ds(0, N - 1)], b_send)
    for rel in range(4):
        for copy in gather_first(rel) + gather_second(rel):
            copy.wait_send()
        for copy in hidden_first(rel) + hidden_second(rel):
            copy.wait_send()
        for s in range(2):
            for copy in scatter_first(s, rel) + scatter_own(s, rel) + scatter_joint(s, rel):
                copy.wait_send()


def on_device(
    child_feat, parent_feat, child_parent, owner, log_gate, norm_gain, w_query, w_key, w_value,
    head_gain, w_out, ffn_gain, w_up, w_down,
):
    vmem = pl.BlockSpec(memory_space=pltpu.VMEM)
    anywhere = pl.BlockSpec(memory_space=pl.ANY)
    dma = pltpu.SemaphoreType.DMA
    return pl.pallas_call(
        kernel,
        out_shape=jax.ShapeDtypeStruct((TOK, Q), BF16),
        in_specs=[
            anywhere, anywhere, vmem, vmem, vmem, vmem, anywhere, anywhere, anywhere, vmem,
            anywhere, vmem, anywhere, anywhere,
        ],
        out_specs=vmem,
        scratch_shapes=[
            pltpu.VMEM((TOK, Q), BF16),
            pltpu.VMEM((PAR, Q), BF16),
            pltpu.VMEM((D, 3 * Q), BF16),
            pltpu.VMEM((Q, D), BF16),
            pltpu.VMEM((D, D), BF16),
            pltpu.VMEM((D, D), BF16),
            pltpu.VMEM((TOK, Q), BF16),
            pltpu.VMEM((TOK, SLOT), BF16),
            pltpu.VMEM((N, CAP, Q), BF16),
            pltpu.VMEM((4, N, CAP, Q), BF16),
            pltpu.VMEM((CH, D), BF16),
            pltpu.VMEM((4, CH, 3 * Q), BF16),
            pltpu.VMEM((4, CH, Q), F32),
            pltpu.VMEM((4, CH, HEADS), F32),
            pltpu.VMEM((4, HEADS, CH), F32),
            pltpu.VMEM((4, Q, Q), F32),
            pltpu.VMEM((4, 1, Q), F32),
            pltpu.VMEM((N, 1, Q + 128), F32),
            pltpu.VMEM((N, 1, Q + 128), F32),
            pltpu.VMEM((N, 1, Q), F32),
            pltpu.VMEM((N, 1, Q), F32),
            pltpu.VMEM((N, CAP, Q), BF16),
            pltpu.VMEM((N, CAP, Q), BF16),
            pltpu.VMEM((2, 4, 4, ROWS, Q), BF16),
            pltpu.VMEM((2, 4, 2, HALF, Q), BF16),
            pltpu.VMEM((2, 4, 2, HALF, Q), BF16),
            pltpu.VMEM((2, 4, 2, 2, HALF, Q), BF16),
            pltpu.VMEM((4, ROWS, Q), F32),
            pltpu.VMEM((4, 4, ROWS, Q), BF16),
            dma((8,)),
            dma,
            dma((4,)),
            dma((4, 4)),
            dma((4, 4)),
            dma, dma, dma, dma, dma, dma,
            dma((2, 4, 2)),
            dma((2, 4, 2)),
            dma((2, 4, 2, 2)),
            dma((2, 4, 2, 2)),
            dma((4, 4)),
            dma((4, 4)),
        ],
        compiler_params=pltpu.CompilerParams(
            collective_id=0, has_side_effects=True, vmem_limit_bytes=56 * 1024 * 1024
        ),
        name="block",
    )(
        child_feat,
        parent_feat,
        child_parent.reshape(1, TOK),
        owner.reshape(1, TOK),
        log_gate,
        norm_gain.reshape(1, D),
        w_query,
        w_key,
        w_value,
        head_gain.reshape(1, Q),
        w_out,
        ffn_gain.reshape(1, D),
        w_up,
        w_down,
    )


def solution(mesh):
    seq, ffn = "seq", "ffn"
    in_specs = (
        P(seq, None), P(seq, None), P(seq), P(seq, None), P(ffn, seq), P(), P(None, ffn),
        P(None, ffn), P(None, ffn), P(ffn), P(ffn, None), P(), P(None, ffn), P(ffn, None),
    )
    return jax.shard_map(
        on_device, mesh=mesh, in_specs=in_specs, out_specs=P(seq, ffn), check_vma=False
    )
```

```python
import jax
import jax.numpy as jnp
from jax import lax
from jax.experimental import pallas as pl
from jax.experimental.pallas import tpu as pltpu
from jax.sharding import PartitionSpec as P

D = 1024
HD = 64
HEADS = 4
Q = 256
TOK = 512
PAR = 64
SLOT = 1024
N = 64
CAP = 16
GRP = 16
CH = 256
ROWS = 128
HALF = 64
EPS = 1e-05
F32 = jnp.float32
BF16 = jnp.bfloat16
MESH = pl.DeviceIdType.MESH
EXACT = lax.Precision.HIGHEST
REL = (0, 1, 3, 2)
AHEAD = 2


def nt(a, b, precision=None):
    return lax.dot_general(
        a, b, (((1,), (1,)), ((), ())), precision=precision, preferred_element_type=F32
    )


def tn(a, b):
    return lax.dot_general(a, b, (((0,), (0,)), ((), ())), preferred_element_type=F32)


def nn(a, b, precision=None):
    return jnp.dot(a, b, precision=precision, preferred_element_type=F32)


def iota(shape, dim):
    return lax.broadcasted_iota(jnp.int32, shape, dim)


def kernel(
    child, parent, cp_row, own_row, gate, ngain, wq, wk, wv, hgain, wo, fgain, wu, wd,
    out,
    child_v, parent_v, wqkv, wo_v, wu_v, wd_v,
    joined, pick_t, outgoing, slots, normed, qkv, att, ccol, crow, loc, offs,
    s_send, s_recv, p_send, p_recv, heads_out, back,
    part, via, comb, fin, hid, hb,
    in_sem, a_send, a_recv, g_send, g_recv, st_send, st_recv, pf_send, pf_recv, b_send, b_recv,
    v_send, v_recv, f_send, f_recv, h_send, h_recv, w_send, w_recv,
):
    me = lax.axis_index("seq")
    fx = lax.axis_index("ffn")
    my_y = me // GRP
    my_zc = me % GRP
    left, right, far = (fx + 3) % 4, (fx + 1) % 4, (fx + 2) % 4

    cols = pl.ds(pl.multiple_of(fx * Q, Q), Q)
    loads = [
        (child, child_v),
        (parent, parent_v),
        (wq, wqkv.at[:, pl.ds(0, Q)]),
        (wk, wqkv.at[:, pl.ds(Q, Q)]),
        (wv, wqkv.at[:, pl.ds(2 * Q, Q)]),
        (wo, wo_v.at[fx]),
        (wu, wu_v),
        (wd, wd_v),
    ]
    loads = [pltpu.make_async_copy(s, d, in_sem.at[i]) for i, (s, d) in enumerate(loads)]
    for copy in loads:
        copy.start()

    barrier = pltpu.get_barrier_semaphore()

    def greet(k, _):
        pl.semaphore_signal(
            barrier, inc=1, device_id=((me + k) % N, fx), device_id_type=MESH
        )
        return 0

    lax.fori_loop(1, N, greet, 0)
    for k in (1, 2, 3):
        pl.semaphore_signal(barrier, inc=1, device_id=(me, (fx + k) % 4), device_id_type=MESH)

    owners = own_row[...]
    member = iota((N, TOK), 0) == owners
    matched = member.astype(F32)
    upper = (iota((TOK, TOK), 0) <= iota((TOK, TOK), 1)).astype(F32).astype(BF16)
    counts = nn(matched.astype(BF16), upper)
    within = jnp.sum(matched * (counts - 1.0), axis=0, keepdims=True)
    target = owners.astype(F32) * float(CAP) + within
    eye = (iota((TOK, TOK), 0) == iota((TOK, TOK), 1)).astype(F32)
    target_col = nt(eye, jnp.broadcast_to(target, (8, TOK)), EXACT)[:, 0:1]
    pick_t[...] = (
        (iota((TOK, SLOT), 1) == (target_col + 0.5).astype(jnp.int32)).astype(F32).astype(BF16)
    )
    parents = (iota((PAR, TOK), 0) == cp_row[...]).astype(F32).astype(BF16)
    loads[0].wait()
    loads[1].wait()
    joined[...] = (child_v[...].astype(F32) + tn(parents, parent_v[...])).astype(BF16)
    target_int = (target + 0.5).astype(jnp.int32)
    for i in range(4):
        pick = (iota((CH, TOK), 0) + i * CH == target_int).astype(F32).astype(BF16)
        outgoing[pl.ds(i * GRP, GRP)] = (
            nn(pick, joined[:, cols]).astype(BF16).reshape(GRP, CAP, Q)
        )

    pl.semaphore_wait(barrier, N - 1 + 3)

    def slot_copy(dest, rel):
        return pltpu.make_async_remote_copy(
            src_ref=outgoing.at[dest],
            dst_ref=slots.at[fx, me],
            send_sem=a_send,
            recv_sem=a_recv.at[(4 - rel) % 4],
            device_id=(dest, fx),
            device_id_type=MESH,
        )

    own_slots = pltpu.make_async_copy(outgoing.at[me], slots.at[fx, me], a_recv.at[0])
    own_slots.start()

    def send_group(rel):
        base = (my_y + rel) % 4 * GRP

        def send(j, _):
            half = (j + 1) // 2
            off = half * (j % 2) + (GRP - half) * (1 - j % 2)
            slot_copy(base + (my_zc + off) % GRP, rel).start()
            return 0

        lax.fori_loop(1 if rel == 0 else 0, GRP, send, 0)

    for rel in REL[:AHEAD]:
        send_group(rel)

    causal = iota((CH, CH), 0) >= iota((CH, CH), 1)
    tri = causal.astype(F32)
    lane_head = iota((1, Q), 1) // HD

    def spread(columns):
        wide = jnp.zeros((columns.shape[0], Q), F32)
        for h in range(HEADS):
            wide = jnp.where(lane_head == h, columns[:, h : h + 1], wide)
        return wide

    block_end = jnp.zeros((1, HEADS), F32)
    for y in range(4):
        g = gate[:, pl.ds(y * CH, CH)]
        crow[y] = nt(g, tri, EXACT)
        columns = nt(tri, g, EXACT)
        ccol[y] = columns
        offs[y] = spread(block_end)
        block_end = block_end + columns[CH - 1 : CH, :]

    def ring(src, dst, send_sem, recv_sem, to):
        return pltpu.make_async_remote_copy(
            src_ref=src, dst_ref=dst, send_sem=send_sem, recv_sem=recv_sem,
            device_id=(me, to), device_id_type=MESH,
        )

    def gather_first(rel):
        rows = pl.ds((my_y + rel) % 4 * GRP, GRP)
        mine = slots.at[fx, rows]
        return [
            ring(mine, mine, g_send.at[rel, 0], g_recv.at[rel, 0], right),
            ring(mine, mine, g_send.at[rel, 1], g_recv.at[rel, 1], left),
        ]

    def gather_second(rel):
        start = (my_y + rel) % 4 * GRP
        a = slots.at[left, pl.ds(start, GRP // 2)]
        b = slots.at[right, pl.ds(start + GRP // 2, GRP // 2)]
        return [
            ring(a, a, g_send.at[rel, 2], g_recv.at[rel, 2], right),
            ring(b, b, g_send.at[rel, 3], g_recv.at[rel, 3], left),
        ]

    def slots_in(rel):
        here = slots.at[fx, pl.ds((my_y + rel) % 4 * GRP, GRP)]
        pltpu.make_async_copy(here, here, a_recv.at[rel]).wait()
        for copy in gather_first(rel):
            copy.start()
        place = REL.index((4 - rel) % 4) + AHEAD
        if place < 4:
            send_group(REL[place])

    def slots_on(rel):
        for copy, after in zip(gather_first(rel), gather_second(rel)):
            copy.wait_recv()
            after.start()

    def project(rel):
        y = (my_y + rel) % 4
        for copy in gather_second(rel):
            copy.wait_recv()
        squares = jnp.zeros((CH, 1), F32)
        for q in range(4):
            x = slots[q, pl.ds(y * GRP, GRP)].reshape(CH, Q).astype(F32)
            squares = squares + jnp.sum(x * x, axis=1, keepdims=True)
        scale = lax.rsqrt(squares / D + EPS)
        for q in range(4):
            x = slots[q, pl.ds(y * GRP, GRP)].reshape(CH, Q).astype(F32)
            gain = ngain[pl.ds(q * Q, Q)].astype(F32).reshape(1, Q)
            normed[:, pl.ds(q * Q, Q)] = (x * scale * gain).astype(BF16)
        qkv[y] = nn(normed[...], wqkv[...]).astype(BF16)

    order = [(4 - rel) % 4 for rel in REL]
    for i in range(6):
        if i < 4:
            slots_in(order[i])
        if 1 <= i < 5:
            slots_on(order[i - 1])
        if i == 1:
            for copy in loads[2:5]:
                copy.wait()
        if i >= 2:
            project(order[i - 2])

    def weights_first():
        mine = wo_v.at[fx]
        return [
            ring(mine, mine, w_send.at[0], w_recv.at[0], right),
            ring(mine, mine, w_send.at[1], w_recv.at[1], left),
        ]

    def weights_second():
        a, b = wo_v.at[left, pl.ds(0, Q // 2)], wo_v.at[right, pl.ds(Q // 2, Q // 2)]
        return [
            ring(a, a, w_send.at[2], w_recv.at[2], right),
            ring(b, b, w_send.at[3], w_recv.at[3], left),
        ]

    loads[5].wait()
    for copy in weights_first():
        copy.start()

    same_head = iota((Q, Q), 0) // HD == iota((Q, Q), 1) // HD
    carried = jnp.zeros((Q, Q), F32)
    for y in range(4):
        loc[y] = carried
        ends = ccol[y, pl.ds(CH - 1, 1), :]
        fade = jnp.exp(spread(ends - ccol[y]))
        added = tn(
            (qkv[y, :, pl.ds(Q, Q)].astype(F32) * fade).astype(BF16),
            qkv[y, :, pl.ds(2 * Q, Q)],
        )
        carried = jnp.exp(spread(ends)) * carried + jnp.where(same_head, added, 0.0)
    state = jnp.zeros((HD, Q), F32)
    for h in range(HEADS):
        state = state + carried[h * HD : (h + 1) * HD, :]
    lane = iota((1, 128), 1)
    ends = jnp.zeros((1, 128), F32)
    for h in range(HEADS):
        ends = jnp.where(lane == h, block_end[:, h : h + 1], ends)
    s_send[:, 0, :] = jnp.concatenate([state, jnp.broadcast_to(ends, (HD, 128))], axis=1)

    def to_all(src, dst, send_sem, recv_sem):
        pltpu.make_async_copy(src.at[me], dst.at[me], recv_sem).start()

        def send(k, _):
            dest = (me + k) % N
            pltpu.make_async_remote_copy(
                src_ref=src.at[dest], dst_ref=dst.at[me], send_sem=send_sem, recv_sem=recv_sem,
                device_id=(dest, fx), device_id_type=MESH,
            ).start()
            return 0

        lax.fori_loop(1, N, send, 0)

    def arrived(ref, sem):
        pltpu.make_async_copy(ref, ref, sem).wait()

    to_all(s_send, s_recv, st_send, st_recv)

    def inside(y):
        q = qkv[y, :, pl.ds(0, Q)]
        k = qkv[y, :, pl.ds(Q, Q)]
        v = qkv[y, :, pl.ds(2 * Q, Q)]
        total = jnp.zeros((CH, Q), F32)
        for h in range(HEADS):
            mine = (lane_head == h).astype(F32).astype(BF16)
            scores = nt(q * mine, k)
            spacing = ccol[y, :, pl.ds(h, 1)] - crow[y, pl.ds(h, 1), :]
            decay = jnp.where(causal, jnp.exp(jnp.minimum(spacing, 0.0)), 0.0)
            total = total + nn((scores * decay).astype(BF16), v * mine)
        att[y] = total

    inside(0)
    inside(1)
    arrived(s_recv, st_recv)
    got = s_recv[:, 0, :]
    got_ends = got[:, Q:]
    states = got[:, :Q]
    tri_n = (iota((N, N), 0) >= iota((N, N), 1)).astype(F32)
    upto = nn(tri_n, got_ends, EXACT)
    before = upto - got_ends
    upto_t = upto.T
    earlier = iota((N, N), 0) > iota((N, N), 1)
    prefix = jnp.zeros((N, Q), F32)
    for h in range(HEADS):
        spacing = before[:, h : h + 1] - upto_t[h : h + 1, :]
        weight = jnp.where(earlier, jnp.exp(jnp.minimum(spacing, 0.0)), 0.0)
        prefix = jnp.where(lane_head == h, nn(weight, states, EXACT), prefix)
    p_send[:, 0, :] = prefix
    to_all(p_send, p_recv, pf_send, pf_recv)
    inside(2)
    inside(3)
    arrived(p_recv, pf_recv)
    for copy, after in zip(weights_first(), weights_second()):
        copy.wait_recv()
        after.start()
    incoming = p_recv[:, 0, :]
    incoming = jnp.where(same_head, jnp.concatenate([incoming] * HEADS, axis=0), 0.0)

    ones_head = same_head.astype(F32).astype(BF16)
    for rel in REL:
        y = (my_y + rel) % 4
        at_start = jnp.exp(offs[y]) * incoming + loc[y]
        outside = nn(qkv[y, :, pl.ds(0, Q)], at_start.astype(BF16))
        o = att[y] + jnp.exp(spread(ccol[y])) * outside
        squares = o * o
        high = squares.astype(BF16)
        low = (squares - high.astype(F32)).astype(BF16)
        mean = (nn(high, ones_head) + nn(low, ones_head)) / HD
        o = o * lax.rsqrt(mean + EPS) * hgain[...].astype(F32).reshape(1, Q)
        heads_out[pl.ds(y * GRP, GRP)] = o.astype(BF16).reshape(GRP, CAP, Q)
        if rel == 0:
            pltpu.make_async_copy(heads_out.at[me], back.at[me], b_recv).start()

        def send(j, _, y=y):
            half = (j + 1) // 2
            off = half * (j % 2) + (GRP - half) * (1 - j % 2)
            dest = y * GRP + (my_zc + off) % GRP
            pltpu.make_async_remote_copy(
                src_ref=heads_out.at[dest], dst_ref=back.at[me], send_sem=b_send, recv_sem=b_recv,
                device_id=(dest, fx), device_id_type=MESH,
            ).start()
            return 0

        lax.fori_loop(1 if rel == 0 else 0, GRP, send, 0)

    top, bottom = pl.ds(0, HALF), pl.ds(HALF, HALF)

    def scatter_first(c):
        return [
            ring(part.at[c, far, top], via.at[c, 0], v_send.at[c, 0], v_recv.at[c, 0], right),
            ring(part.at[c, far, bottom], via.at[c, 1], v_send.at[c, 1], v_recv.at[c, 1], left),
        ]

    def scatter_own(c):
        return [
            ring(part.at[c, right, bottom], fin.at[c, 0, 1], f_send.at[c, 0, 1], f_recv.at[c, 0, 1], right),
            ring(part.at[c, left, top], fin.at[c, 1, 0], f_send.at[c, 1, 0], f_recv.at[c, 1, 0], left),
        ]

    def scatter_joint(c):
        return [
            ring(comb.at[c, 0], fin.at[c, 0, 0], f_send.at[c, 0, 0], f_recv.at[c, 0, 0], right),
            ring(comb.at[c, 1], fin.at[c, 1, 1], f_send.at[c, 1, 1], f_recv.at[c, 1, 1], left),
        ]

    def scatter_start(c, product):
        for q in range(4):
            part[c, q] = product[:, q * Q : (q + 1) * Q].astype(BF16)
        for copy in scatter_first(c) + scatter_own(c):
            copy.start()

    def scatter_on(c):
        pieces = [(right, top), (left, bottom)]
        for d, (copy, after) in enumerate(zip(scatter_first(c), scatter_joint(c))):
            copy.wait_recv()
            whose, rows = pieces[d]
            comb[c, d] = (
                part[c, whose, rows, :].astype(F32) + via[c, d].astype(F32)
            ).astype(BF16)
            after.start()

    def scattered(c):
        for copy in scatter_own(c) + scatter_joint(c):
            copy.wait_recv()
        total = part[c, fx].astype(F32)
        for d in range(2):
            total = total + fin[c, d].reshape(ROWS, Q).astype(F32)
        return total

    def hidden_first(c):
        mine = hb.at[fx, c]
        return [
            ring(mine, mine, h_send.at[c, 0], h_recv.at[c, 0], right),
            ring(mine, mine, h_send.at[c, 1], h_recv.at[c, 1], left),
        ]

    def hidden_second(c):
        a, b = hb.at[left, c, top], hb.at[right, c, bottom]
        return [
            ring(a, a, h_send.at[c, 2], h_recv.at[c, 2], right),
            ring(b, b, h_send.at[c, 3], h_recv.at[c, 3], left),
        ]

    def hidden_on(c):
        for copy, after in zip(hidden_first(c), hidden_second(c)):
            copy.wait_recv()
            after.start()

    def feed_forward(c):
        rows = pl.ds(c * ROWS, ROWS)
        for copy in hidden_second(c):
            copy.wait_recv()
        heads = jnp.concatenate([hb[q, c] for q in range(4)], axis=1)
        hidden = joined[rows, :].astype(F32) + nn(heads, wo_v[...].reshape(D, D))
        for q in range(4):
            hid[c, q] = hidden[:, q * Q : (q + 1) * Q]
        scale = lax.rsqrt(jnp.sum(hidden * hidden, axis=1, keepdims=True) / D + EPS)
        second = (hidden * scale * fgain[...].astype(F32).reshape(1, D)).astype(BF16)
        expanded = jax.nn.gelu(nn(second, wu_v[...])).astype(BF16)
        scatter_start(c, nn(expanded, wd_v[...]))

    def finish(c):
        out[pl.ds(c * ROWS, ROWS), :] = (hid[c, fx] + scattered(c)).astype(BF16)

    arrived(back, b_recv)
    for c in range(4):
        rows = pl.ds(c * ROWS, ROWS)
        hb[fx, c] = nn(pick_t[rows, :], back[...].reshape(SLOT, Q)).astype(BF16)
        for copy in hidden_first(c):
            copy.start()
    for copy in loads[6:]:
        copy.wait()
    for copy in weights_second():
        copy.wait_recv()
    steps = [(0, hidden_on), (1, feed_forward), (3, scatter_on), (4, finish)]
    for i in range(8):
        for delay, step in steps:
            if 0 <= i - delay < 4:
                step(i - delay)

    arrived(outgoing.at[pl.ds(0, N - 1)], a_send)
    arrived(s_send.at[pl.ds(0, N - 1)], st_send)
    arrived(p_send.at[pl.ds(0, N - 1)], pf_send)
    arrived(heads_out.at[pl.ds(0, N - 1)], b_send)
    for rel in range(4):
        for copy in gather_first(rel) + gather_second(rel):
            copy.wait_send()
        for copy in hidden_first(rel) + hidden_second(rel):
            copy.wait_send()
        for copy in scatter_first(rel) + scatter_own(rel) + scatter_joint(rel):
            copy.wait_send()
    for copy in weights_first() + weights_second():
        copy.wait_send()


def on_device(
    child_feat, parent_feat, child_parent, owner, log_gate, norm_gain, w_query, w_key, w_value,
    head_gain, w_out, ffn_gain, w_up, w_down,
):
    vmem = pl.BlockSpec(memory_space=pltpu.VMEM)
    anywhere = pl.BlockSpec(memory_space=pl.ANY)
    dma = pltpu.SemaphoreType.DMA
    return pl.pallas_call(
        kernel,
        out_shape=jax.ShapeDtypeStruct((TOK, Q), BF16),
        in_specs=[
            anywhere, anywhere, vmem, vmem, vmem, vmem, anywhere, anywhere, anywhere, vmem,
            anywhere, vmem, anywhere, anywhere,
        ],
        out_specs=vmem,
        scratch_shapes=[
            pltpu.VMEM((TOK, D), BF16),
            pltpu.VMEM((PAR, D), BF16),
            pltpu.VMEM((D, 3 * Q), BF16),
            pltpu.VMEM((4, Q, D), BF16),
            pltpu.VMEM((D, D), BF16),
            pltpu.VMEM((D, D), BF16),
            pltpu.VMEM((TOK, D), BF16),
            pltpu.VMEM((TOK, SLOT), BF16),
            pltpu.VMEM((N, CAP, Q), BF16),
            pltpu.VMEM((4, N, CAP, Q), BF16),
            pltpu.VMEM((CH, D), BF16),
            pltpu.VMEM((4, CH, 3 * Q), BF16),
            pltpu.VMEM((4, CH, Q), F32),
            pltpu.VMEM((4, CH, HEADS), F32),
            pltpu.VMEM((4, HEADS, CH), F32),
            pltpu.VMEM((4, Q, Q), F32),
            pltpu.VMEM((4, 1, Q), F32),
            pltpu.VMEM((N, 1, Q + 128), F32),
            pltpu.VMEM((N, 1, Q + 128), F32),
            pltpu.VMEM((N, 1, Q), F32),
            pltpu.VMEM((N, 1, Q), F32),
            pltpu.VMEM((N, CAP, Q), BF16),
            pltpu.VMEM((N, CAP, Q), BF16),
            pltpu.VMEM((4, 4, ROWS, Q), BF16),
            pltpu.VMEM((4, 2, HALF, Q), BF16),
            pltpu.VMEM((4, 2, HALF, Q), BF16),
            pltpu.VMEM((4, 2, 2, HALF, Q), BF16),
            pltpu.VMEM((4, 4, ROWS, Q), F32),
            pltpu.VMEM((4, 4, ROWS, Q), BF16),
            dma((8,)),
            dma,
            dma((4,)),
            dma((4, 4)),
            dma((4, 4)),
            dma, dma, dma, dma, dma, dma,
            dma((4, 2)),
            dma((4, 2)),
            dma((4, 2, 2)),
            dma((4, 2, 2)),
            dma((4, 4)),
            dma((4, 4)),
            dma((4,)),
            dma((4,)),
        ],
        compiler_params=pltpu.CompilerParams(
            collective_id=0, has_side_effects=True, vmem_limit_bytes=56 * 1024 * 1024
        ),
        name="block",
    )(
        child_feat,
        parent_feat,
        child_parent.reshape(1, TOK),
        owner.reshape(1, TOK),
        log_gate,
        norm_gain,
        w_query,
        w_key,
        w_value,
        head_gain,
        w_out,
        ffn_gain,
        w_up,
        w_down,
    )


def solution(mesh):
    seq, ffn = "seq", "ffn"
    in_specs = (
        P(seq, None), P(seq, None), P(seq), P(seq, None), P(ffn, seq), P(), P(None, ffn),
        P(None, ffn), P(None, ffn), P(ffn), P(ffn, None), P(), P(None, ffn), P(ffn, None),
    )
    return jax.shard_map(
        on_device, mesh=mesh, in_specs=in_specs, out_specs=P(seq, ffn), check_vma=False
    )
```

```python
import jax
import jax.numpy as jnp
from jax import lax
from jax.experimental import pallas as pl
from jax.experimental.pallas import tpu as pltpu
from jax.sharding import PartitionSpec as P

D = 1024
HD = 64
HEADS = 4
Q = 256
TOK = 512
PAR = 64
SLOT = 1024
N = 64
CAP = 16
GRP = 16
CH = 256
PARTS = 4
ROWS = TOK // PARTS
HALF = ROWS // 2
GATHER_DIRECT = (0,)
SCATTER_DIRECT = (PARTS - 1,)
EPS = 1e-05
F32 = jnp.float32
BF16 = jnp.bfloat16
MESH = pl.DeviceIdType.MESH
EXACT = lax.Precision.HIGHEST
REL = (2, 1, 3, 0)
AHEAD = 2


def nt(a, b, precision=None):
    return lax.dot_general(
        a, b, (((1,), (1,)), ((), ())), precision=precision, preferred_element_type=F32
    )


def tn(a, b):
    return lax.dot_general(a, b, (((0,), (0,)), ((), ())), preferred_element_type=F32)


def nn(a, b, precision=None):
    return jnp.dot(a, b, precision=precision, preferred_element_type=F32)


def farthest_first(j):
    return GRP // 2 + (j + 1) // 2 * (2 * (j % 2) - 1)


def iota(shape, dim):
    return lax.broadcasted_iota(jnp.int32, shape, dim)


def kernel(
    child, parent, cp_row, own_row, gate, ngain, wq, wk, wv, hgain, wo, fgain, wu, wd,
    out,
    child_q, parent_q, child_v, parent_v, wqkv, wo_v, wu_v, wd_v,
    joined, pick_t, outgoing, slots, normed, qkv, att, ccol, crow, loc, offs,
    s_send, s_recv, p_send, p_recv, t_send, t_recv, heads_out, back,
    part, via, comb, fin, hid, hb,
    in_sem, a_send, a_recv, g_send, g_recv, st_send, st_recv, pf_send, pf_recv, b_send, b_recv,
    v_send, v_recv, f_send, f_recv, h_send, h_recv, w_send, w_recv, t_sent, t_got,
):
    me = lax.axis_index("seq")
    fx = lax.axis_index("ffn")
    my_y = me // GRP
    my_zc = me % GRP
    left, right, far = (fx + 3) % 4, (fx + 1) % 4, (fx + 2) % 4

    cols = pl.ds(pl.multiple_of(fx * Q, Q), Q)
    loads = [
        (child.at[:, cols], child_q),
        (parent.at[:, cols], parent_q),
        (child, child_v),
        (parent, parent_v),
        (wq, wqkv.at[:, pl.ds(0, Q)]),
        (wk, wqkv.at[:, pl.ds(Q, Q)]),
        (wv, wqkv.at[:, pl.ds(2 * Q, Q)]),
        (wo, wo_v.at[fx]),
        (wu, wu_v),
        (wd, wd_v),
    ]
    loads = [pltpu.make_async_copy(s, d, in_sem.at[i]) for i, (s, d) in enumerate(loads)]
    for copy in loads[:2]:
        copy.start()

    barrier = pltpu.get_barrier_semaphore()

    def greet(k, _):
        pl.semaphore_signal(
            barrier, inc=1, device_id=((me + k) % N, fx), device_id_type=MESH
        )
        return 0

    lax.fori_loop(1, N, greet, 0)
    for k in (1, 2, 3):
        pl.semaphore_signal(barrier, inc=1, device_id=(me, (fx + k) % 4), device_id_type=MESH)

    owners = own_row[...]
    matched = (iota((N, TOK), 0) == owners).astype(F32)
    upper = (iota((TOK, TOK), 0) <= iota((TOK, TOK), 1)).astype(F32).astype(BF16)
    counts = nn(matched.astype(BF16), upper)
    within = jnp.sum(matched * (counts - 1.0), axis=0, keepdims=True)
    target = owners.astype(F32) * float(CAP) + within
    target_int = (target + 0.5).astype(jnp.int32)
    parents = (iota((PAR, TOK), 0) == cp_row[...]).astype(F32).astype(BF16)
    loads[0].wait()
    loads[1].wait()
    for copy in loads[2:]:
        copy.start()
    quarter = (child_q[...].astype(F32) + tn(parents, parent_q[...])).astype(BF16)

    def slot_copy(dest, rel):
        return pltpu.make_async_remote_copy(
            src_ref=outgoing.at[dest],
            dst_ref=slots.at[fx, me],
            send_sem=a_send,
            recv_sem=a_recv.at[(4 - rel) % 4],
            device_id=(dest, fx),
            device_id_type=MESH,
        )

    def place_group(rel):
        y = (my_y + rel) % 4
        pick = (iota((CH, TOK), 0) + y * CH == target_int).astype(F32).astype(BF16)
        outgoing[pl.ds(y * GRP, GRP)] = nn(pick, quarter).astype(BF16).reshape(GRP, CAP, Q)

    def send_group(rel):
        base = (my_y + rel) % 4 * GRP
        if rel == 0:
            pltpu.make_async_copy(outgoing.at[me], slots.at[fx, me], a_recv.at[0]).start()

        def send(j, _):
            slot_copy(base + (my_zc + farthest_first(j)) % GRP, rel).start()
            return 0

        lax.fori_loop(0, GRP - 1 if rel == 0 else GRP, send, 0)

    place_group(REL[0])
    pl.semaphore_wait(barrier, N - 1 + 3)
    send_group(REL[0])
    for rel in REL[1:]:
        place_group(rel)
        if REL.index(rel) < AHEAD:
            send_group(rel)

    eye = (iota((TOK, TOK), 0) == iota((TOK, TOK), 1)).astype(F32)
    target_col = nt(eye, jnp.broadcast_to(target, (8, TOK)), EXACT)[:, 0:1]
    pick_t[...] = (
        (iota((TOK, SLOT), 1) == (target_col + 0.5).astype(jnp.int32)).astype(F32).astype(BF16)
    )
    loads[2].wait()
    loads[3].wait()
    joined[...] = (child_v[...].astype(F32) + tn(parents, parent_v[...])).astype(BF16)

    causal = iota((CH, CH), 0) >= iota((CH, CH), 1)
    tri = causal.astype(F32)
    lane_head = iota((1, Q), 1) // HD

    def spread(columns):
        wide = jnp.zeros((columns.shape[0], Q), F32)
        for h in range(HEADS):
            wide = jnp.where(lane_head == h, columns[:, h : h + 1], wide)
        return wide

    block_end = jnp.zeros((1, HEADS), F32)
    for y in range(4):
        g = gate[:, pl.ds(y * CH, CH)]
        crow[y] = nt(g, tri, EXACT)
        columns = nt(tri, g, EXACT)
        ccol[y] = columns
        offs[y] = spread(block_end)
        block_end = block_end + columns[CH - 1 : CH, :]

    def ring(src, dst, send_sem, recv_sem, to):
        return pltpu.make_async_remote_copy(
            src_ref=src, dst_ref=dst, send_sem=send_sem, recv_sem=recv_sem,
            device_id=(me, to), device_id_type=MESH,
        )

    def gather_first(rel):
        rows = pl.ds((my_y + rel) % 4 * GRP, GRP)
        mine = slots.at[fx, rows]
        return [
            ring(mine, mine, g_send.at[rel, 0], g_recv.at[rel, 0], right),
            ring(mine, mine, g_send.at[rel, 1], g_recv.at[rel, 1], left),
        ]

    def gather_second(rel):
        start = (my_y + rel) % 4 * GRP
        a = slots.at[left, pl.ds(start, GRP // 2)]
        b = slots.at[right, pl.ds(start + GRP // 2, GRP // 2)]
        return [
            ring(a, a, g_send.at[rel, 2], g_recv.at[rel, 2], right),
            ring(b, b, g_send.at[rel, 3], g_recv.at[rel, 3], left),
        ]

    def slots_in(rel):
        here = slots.at[fx, pl.ds((my_y + rel) % 4 * GRP, GRP)]
        pltpu.make_async_copy(here, here, a_recv.at[rel]).wait()
        for copy in gather_first(rel):
            copy.start()
        place = REL.index((4 - rel) % 4) + AHEAD
        if place < 4:
            send_group(REL[place])

    def slots_on(rel):
        for copy, after in zip(gather_first(rel), gather_second(rel)):
            copy.wait_recv()
            after.start()

    def project(rel):
        y = (my_y + rel) % 4
        for copy in gather_second(rel):
            copy.wait_recv()
        squares = jnp.zeros((CH, 1), F32)
        for q in range(4):
            x = slots[q, pl.ds(y * GRP, GRP)].reshape(CH, Q).astype(F32)
            squares = squares + jnp.sum(x * x, axis=1, keepdims=True)
        scale = lax.rsqrt(squares / D + EPS)
        for q in range(4):
            x = slots[q, pl.ds(y * GRP, GRP)].reshape(CH, Q).astype(F32)
            gain = ngain[pl.ds(q * Q, Q)].astype(F32).reshape(1, Q)
            normed[:, pl.ds(q * Q, Q)] = (x * scale * gain).astype(BF16)
        qkv[y] = nn(normed[...], wqkv[...]).astype(BF16)

    order = [(4 - rel) % 4 for rel in REL]
    for i in range(6):
        if i < 4:
            slots_in(order[i])
        if 1 <= i < 5:
            slots_on(order[i - 1])
        if i == 1:
            for copy in loads[4:7]:
                copy.wait()
        if i >= 2:
            project(order[i - 2])

    def weights_first():
        mine = wo_v.at[fx]
        return [
            ring(mine, mine, w_send.at[0], w_recv.at[0], right),
            ring(mine, mine, w_send.at[1], w_recv.at[1], left),
        ]

    def weights_second():
        a, b = wo_v.at[left, pl.ds(0, Q // 2)], wo_v.at[right, pl.ds(Q // 2, Q // 2)]
        return [
            ring(a, a, w_send.at[2], w_recv.at[2], right),
            ring(b, b, w_send.at[3], w_recv.at[3], left),
        ]

    loads[7].wait()
    for copy in weights_first():
        copy.start()

    same_head = iota((Q, Q), 0) // HD == iota((Q, Q), 1) // HD
    carried = jnp.zeros((Q, Q), F32)
    for y in range(4):
        loc[y] = carried
        ends = ccol[y, pl.ds(CH - 1, 1), :]
        fade = jnp.exp(spread(ends - ccol[y]))
        added = tn(
            (qkv[y, :, pl.ds(Q, Q)].astype(F32) * fade).astype(BF16),
            qkv[y, :, pl.ds(2 * Q, Q)],
        )
        carried = jnp.exp(spread(ends)) * carried + jnp.where(same_head, added, 0.0)
    state = jnp.zeros((HD, Q), F32)
    for h in range(HEADS):
        state = state + carried[h * HD : (h + 1) * HD, :]
    lane = iota((1, 128), 1)
    ends = jnp.zeros((1, 128), F32)
    for h in range(HEADS):
        ends = jnp.where(lane == h, block_end[:, h : h + 1], ends)
    message = jnp.concatenate([state, jnp.broadcast_to(ends, (HD, 128))], axis=1)
    for r in range(4):
        s_send[:, r, :] = message[r * GRP : (r + 1) * GRP, :]

    def to_row(src, dst, send_sem, recv_sem):
        pltpu.make_async_copy(src.at[my_zc], dst.at[my_zc], recv_sem).start()

        def send(k, _):
            peer = (my_zc + farthest_first(k)) % GRP
            pltpu.make_async_remote_copy(
                src_ref=src.at[peer], dst_ref=dst.at[my_zc], send_sem=send_sem, recv_sem=recv_sem,
                device_id=(my_y * GRP + peer, fx), device_id_type=MESH,
            ).start()
            return 0

        lax.fori_loop(0, GRP - 1, send, 0)

    def totals_to(k):
        return pltpu.make_async_remote_copy(
            src_ref=t_send, dst_ref=t_recv.at[my_y],
            send_sem=t_sent.at[k - 1], recv_sem=t_got.at[k - 1],
            device_id=((my_y + k) % 4 * GRP + my_zc, fx), device_id_type=MESH,
        )

    def arrived(ref, sem):
        pltpu.make_async_copy(ref, ref, sem).wait()

    to_row(s_send, s_recv, st_send, st_recv)

    def inside(y):
        q = qkv[y, :, pl.ds(0, Q)]
        k = qkv[y, :, pl.ds(Q, Q)]
        v = qkv[y, :, pl.ds(2 * Q, Q)]
        total = jnp.zeros((CH, Q), F32)
        for h in range(HEADS):
            mine = (lane_head == h).astype(F32).astype(BF16)
            scores = nt(q * mine, k)
            spacing = ccol[y, :, pl.ds(h, 1)] - crow[y, pl.ds(h, 1), :]
            decay = jnp.where(causal, jnp.exp(jnp.minimum(spacing, 0.0)), 0.0)
            total = total + nn((scores * decay).astype(BF16), v * mine)
        att[y] = total

    inside(0)
    arrived(s_recv, st_recv)
    rows_got = [s_recv[:, r, :] for r in range(4)]
    got_ends = rows_got[0][:, Q:]
    states = jnp.concatenate([row[:, :Q] for row in rows_got], axis=1)
    tri_row = (iota((GRP, GRP), 0) >= iota((GRP, GRP), 1)).astype(F32)
    upto = nn(tri_row, got_ends, EXACT)
    row_end = upto[GRP - 1 :, :]
    before = jnp.concatenate([upto - got_ends, jnp.broadcast_to(row_end, (8, 128))], axis=0)
    upto_t = upto.T
    earlier = iota((GRP + 8, GRP), 0) > iota((GRP + 8, GRP), 1)
    wide_head = iota((1, 4 * Q), 1) // HD % HEADS
    prefix = jnp.zeros((GRP + 8, 4 * Q), F32)
    passing = jnp.zeros((GRP, 4 * Q), F32)
    for h in range(HEADS):
        spacing = before[:, h : h + 1] - upto_t[h : h + 1, :]
        weight = jnp.where(earlier, jnp.exp(jnp.minimum(spacing, 0.0)), 0.0)
        prefix = jnp.where(wide_head == h, nn(weight, states, EXACT), prefix)
        passing = jnp.where(wide_head == h, jnp.exp(before[:GRP, h : h + 1]), passing)
    t_send[...] = jnp.concatenate([prefix[GRP : GRP + 1, :], row_end], axis=1)
    for k in (2, 1, 3):
        totals_to(k).start()
    t_recv[my_y] = t_send[...]
    inside(1)
    for k in (1, 2, 3):
        totals_to(k).wait_recv()
    row_in = jnp.zeros((1, 4 * Q), F32)
    for y in range(3):
        total = t_recv[y]
        fading = jnp.zeros((1, 4 * Q), F32)
        for h in range(HEADS):
            fading = jnp.where(
                wide_head == h, jnp.exp(total[:, 4 * Q + h : 4 * Q + h + 1]), fading
            )
        row_in = jnp.where(y < my_y, fading * row_in + total[:, : 4 * Q], row_in)
    prefix = prefix[:GRP, :] + passing * row_in
    for r in range(4):
        p_send[:, r, :] = prefix[:, r * Q : (r + 1) * Q]
    to_row(p_send, p_recv, pf_send, pf_recv)
    inside(2)
    inside(3)
    arrived(p_recv, pf_recv)
    for copy, after in zip(weights_first(), weights_second()):
        copy.wait_recv()
        after.start()
    incoming = jnp.concatenate([p_recv[:, r, :] for r in range(4)], axis=0)
    incoming = jnp.where(same_head, jnp.concatenate([incoming] * HEADS, axis=0), 0.0)

    ones_head = same_head.astype(F32).astype(BF16)
    for rel in REL:
        y = (my_y + rel) % 4
        at_start = jnp.exp(offs[y]) * incoming + loc[y]
        outside = nn(qkv[y, :, pl.ds(0, Q)], at_start.astype(BF16))
        o = att[y] + jnp.exp(spread(ccol[y])) * outside
        squares = o * o
        high = squares.astype(BF16)
        low = (squares - high.astype(F32)).astype(BF16)
        mean = (nn(high, ones_head) + nn(low, ones_head)) / HD
        o = o * lax.rsqrt(mean + EPS) * hgain[...].astype(F32).reshape(1, Q)
        heads_out[pl.ds(y * GRP, GRP)] = o.astype(BF16).reshape(GRP, CAP, Q)
        if rel == 0:
            pltpu.make_async_copy(heads_out.at[me], back.at[me], b_recv).start()

        def send(j, _, y=y):
            dest = y * GRP + (my_zc + farthest_first(j)) % GRP
            pltpu.make_async_remote_copy(
                src_ref=heads_out.at[dest], dst_ref=back.at[me], send_sem=b_send, recv_sem=b_recv,
                device_id=(dest, fx), device_id_type=MESH,
            ).start()
            return 0

        lax.fori_loop(0, GRP - 1 if rel == 0 else GRP, send, 0)

    top, bottom = pl.ds(0, HALF), pl.ds(HALF, HALF)

    def scatter_first(c):
        if c in SCATTER_DIRECT:
            return [
                ring(part.at[c, far, top], via.at[c, 0], v_send.at[c, 0], v_recv.at[c, 0], far),
                ring(part.at[c, far, bottom], via.at[c, 1], v_send.at[c, 1], v_recv.at[c, 1], far),
            ]
        return [
            ring(part.at[c, far, top], via.at[c, 0], v_send.at[c, 0], v_recv.at[c, 0], right),
            ring(part.at[c, far, bottom], via.at[c, 1], v_send.at[c, 1], v_recv.at[c, 1], left),
        ]

    def scatter_own(c):
        return [
            ring(part.at[c, right, bottom], fin.at[c, 0, 1], f_send.at[c, 0, 1], f_recv.at[c, 0, 1], right),
            ring(part.at[c, left, top], fin.at[c, 1, 0], f_send.at[c, 1, 0], f_recv.at[c, 1, 0], left),
        ]

    def scatter_joint(c):
        if c in SCATTER_DIRECT:
            return [
                ring(part.at[c, right, top], fin.at[c, 0, 0], f_send.at[c, 0, 0], f_recv.at[c, 0, 0], right),
                ring(part.at[c, left, bottom], fin.at[c, 1, 1], f_send.at[c, 1, 1], f_recv.at[c, 1, 1], left),
            ]
        return [
            ring(comb.at[c, 0], fin.at[c, 0, 0], f_send.at[c, 0, 0], f_recv.at[c, 0, 0], right),
            ring(comb.at[c, 1], fin.at[c, 1, 1], f_send.at[c, 1, 1], f_recv.at[c, 1, 1], left),
        ]

    def scatter_start(c, product):
        for q in range(4):
            part[c, q] = product[:, q * Q : (q + 1) * Q].astype(BF16)
        for copy in scatter_first(c) + scatter_own(c):
            copy.start()
        if c in SCATTER_DIRECT:
            for copy in scatter_joint(c):
                copy.start()

    def scatter_on(c):
        if c in SCATTER_DIRECT:
            return
        pieces = [(right, top), (left, bottom)]
        for d, (copy, after) in enumerate(zip(scatter_first(c), scatter_joint(c))):
            copy.wait_recv()
            whose, rows = pieces[d]
            comb[c, d] = (
                part[c, whose, rows, :].astype(F32) + via[c, d].astype(F32)
            ).astype(BF16)
            after.start()

    def scattered(c):
        for copy in scatter_own(c) + scatter_joint(c):
            copy.wait_recv()
        total = part[c, fx].astype(F32)
        if c in SCATTER_DIRECT:
            for copy in scatter_first(c):
                copy.wait_recv()
            total = total + via[c].reshape(ROWS, Q).astype(F32)
        for d in range(2):
            total = total + fin[c, d].reshape(ROWS, Q).astype(F32)
        return total

    def hidden_first(c):
        mine = hb.at[fx, c]
        return [
            ring(mine, mine, h_send.at[c, 0], h_recv.at[c, 0], right),
            ring(mine, mine, h_send.at[c, 1], h_recv.at[c, 1], left),
        ]

    def hidden_second(c):
        if c in GATHER_DIRECT:
            mine = hb.at[fx, c]
            return [ring(mine, mine, h_send.at[c, 2], h_recv.at[c, 2], far)]
        a, b = hb.at[left, c, top], hb.at[right, c, bottom]
        return [
            ring(a, a, h_send.at[c, 2], h_recv.at[c, 2], right),
            ring(b, b, h_send.at[c, 3], h_recv.at[c, 3], left),
        ]

    def hidden_on(c):
        if c in GATHER_DIRECT:
            for copy in hidden_first(c):
                copy.wait_recv()
            return
        for copy, after in zip(hidden_first(c), hidden_second(c)):
            copy.wait_recv()
            after.start()

    def feed_forward(c):
        rows = pl.ds(c * ROWS, ROWS)
        for copy in hidden_second(c):
            copy.wait_recv()
        heads = jnp.concatenate([hb[q, c] for q in range(4)], axis=1)
        hidden = joined[rows, :].astype(F32) + nn(heads, wo_v[...].reshape(D, D))
        for q in range(4):
            hid[c, q] = hidden[:, q * Q : (q + 1) * Q]
        scale = lax.rsqrt(jnp.sum(hidden * hidden, axis=1, keepdims=True) / D + EPS)
        second = (hidden * scale * fgain[...].astype(F32).reshape(1, D)).astype(BF16)
        expanded = jax.nn.gelu(nn(second, wu_v[...])).astype(BF16)
        scatter_start(c, nn(expanded, wd_v[...]))

    def finish(c):
        out[pl.ds(c * ROWS, ROWS), :] = (hid[c, fx] + scattered(c)).astype(BF16)

    arrived(back, b_recv)
    for c in range(PARTS):
        rows = pl.ds(c * ROWS, ROWS)
        hb[fx, c] = nn(pick_t[rows, :], back[...].reshape(SLOT, Q)).astype(BF16)
        for copy in hidden_first(c) + (hidden_second(c) if c in GATHER_DIRECT else []):
            copy.start()
    for copy in loads[8:]:
        copy.wait()
    for copy in weights_second():
        copy.wait_recv()
    steps = [(0, hidden_on), (1, feed_forward), (3, scatter_on), (4, finish)]
    for i in range(PARTS + 4):
        for delay, step in steps:
            if 0 <= i - delay < PARTS:
                step(i - delay)

    arrived(outgoing.at[pl.ds(0, N - 1)], a_send)
    arrived(s_send.at[pl.ds(0, GRP - 1)], st_send)
    arrived(p_send.at[pl.ds(0, GRP - 1)], pf_send)
    for k in (1, 2, 3):
        totals_to(k).wait_send()
    arrived(heads_out.at[pl.ds(0, N - 1)], b_send)
    for rel in range(4):
        for copy in gather_first(rel) + gather_second(rel):
            copy.wait_send()
    for c in range(PARTS):
        for copy in hidden_first(c) + hidden_second(c):
            copy.wait_send()
        for copy in scatter_first(c) + scatter_own(c) + scatter_joint(c):
            copy.wait_send()
    for copy in weights_first() + weights_second():
        copy.wait_send()


def on_device(
    child_feat, parent_feat, child_parent, owner, log_gate, norm_gain, w_query, w_key, w_value,
    head_gain, w_out, ffn_gain, w_up, w_down,
):
    vmem = pl.BlockSpec(memory_space=pltpu.VMEM)
    anywhere = pl.BlockSpec(memory_space=pl.ANY)
    dma = pltpu.SemaphoreType.DMA
    return pl.pallas_call(
        kernel,
        out_shape=jax.ShapeDtypeStruct((TOK, Q), BF16),
        in_specs=[
            anywhere, anywhere, vmem, vmem, vmem, vmem, anywhere, anywhere, anywhere, vmem,
            anywhere, vmem, anywhere, anywhere,
        ],
        out_specs=vmem,
        scratch_shapes=[
            pltpu.VMEM((TOK, Q), BF16),
            pltpu.VMEM((PAR, Q), BF16),
            pltpu.VMEM((TOK, D), BF16),
            pltpu.VMEM((PAR, D), BF16),
            pltpu.VMEM((D, 3 * Q), BF16),
            pltpu.VMEM((4, Q, D), BF16),
            pltpu.VMEM((D, D), BF16),
            pltpu.VMEM((D, D), BF16),
            pltpu.VMEM((TOK, D), BF16),
            pltpu.VMEM((TOK, SLOT), BF16),
            pltpu.VMEM((N, CAP, Q), BF16),
            pltpu.VMEM((4, N, CAP, Q), BF16),
            pltpu.VMEM((CH, D), BF16),
            pltpu.VMEM((4, CH, 3 * Q), BF16),
            pltpu.VMEM((4, CH, Q), F32),
            pltpu.VMEM((4, CH, HEADS), F32),
            pltpu.VMEM((4, HEADS, CH), F32),
            pltpu.VMEM((4, Q, Q), F32),
            pltpu.VMEM((4, 1, Q), F32),
            pltpu.VMEM((GRP, 4, Q + 128), F32),
            pltpu.VMEM((GRP, 4, Q + 128), F32),
            pltpu.VMEM((GRP, 4, Q), F32),
            pltpu.VMEM((GRP, 4, Q), F32),
            pltpu.VMEM((1, 4 * Q + 128), F32),
            pltpu.VMEM((4, 1, 4 * Q + 128), F32),
            pltpu.VMEM((N, CAP, Q), BF16),
            pltpu.VMEM((N, CAP, Q), BF16),
            pltpu.VMEM((PARTS, 4, ROWS, Q), BF16),
            pltpu.VMEM((PARTS, 2, HALF, Q), BF16),
            pltpu.VMEM((PARTS, 2, HALF, Q), BF16),
            pltpu.VMEM((PARTS, 2, 2, HALF, Q), BF16),
            pltpu.VMEM((PARTS, 4, ROWS, Q), F32),
            pltpu.VMEM((4, PARTS, ROWS, Q), BF16),
            dma((10,)),
            dma,
            dma((4,)),
            dma((4, 4)),
            dma((4, 4)),
            dma, dma, dma, dma, dma, dma,
            dma((PARTS, 2)),
            dma((PARTS, 2)),
            dma((PARTS, 2, 2)),
            dma((PARTS, 2, 2)),
            dma((PARTS, 4)),
            dma((PARTS, 4)),
            dma((4,)),
            dma((4,)),
            dma((3,)),
            dma((3,)),
        ],
        compiler_params=pltpu.CompilerParams(
            collective_id=0, has_side_effects=True, vmem_limit_bytes=56 * 1024 * 1024
        ),
        name="block",
    )(
        child_feat,
        parent_feat,
        child_parent.reshape(1, TOK),
        owner.reshape(1, TOK),
        log_gate,
        norm_gain,
        w_query,
        w_key,
        w_value,
        head_gain,
        w_out,
        ffn_gain,
        w_up,
        w_down,
    )


def solution(mesh):
    seq, ffn = "seq", "ffn"
    in_specs = (
        P(seq, None), P(seq, None), P(seq), P(seq, None), P(ffn, seq), P(), P(None, ffn),
        P(None, ffn), P(None, ffn), P(ffn), P(ffn, None), P(), P(None, ffn), P(ffn, None),
    )
    return jax.shard_map(
        on_device, mesh=mesh, in_specs=in_specs, out_specs=P(seq, ffn), check_vma=False
    )
```

```python
import jax
import jax.numpy as jnp
from jax import lax
from jax.experimental import pallas as pl
from jax.experimental.pallas import tpu as pltpu
from jax.sharding import PartitionSpec as P

D = 1024
HD = 64
HEADS = 4
Q = 256
TOK = 512
PAR = 64
SLOT = 1024
N = 64
CAP = 16
GRP = 16
CH = 256
PARTS = 4
ROWS = TOK // PARTS
HALF = ROWS // 2
GATHER_DIRECT = (0,)
SCATTER_DIRECT = (PARTS - 1,)
EPS = 1e-05
F32 = jnp.float32
BF16 = jnp.bfloat16
MESH = pl.DeviceIdType.MESH
EXACT = lax.Precision.HIGHEST
REL = (2, 1, 3, 0)
AHEAD = 2


def nt(a, b, precision=None):
    return lax.dot_general(
        a, b, (((1,), (1,)), ((), ())), precision=precision, preferred_element_type=F32
    )


def tn(a, b):
    return lax.dot_general(a, b, (((0,), (0,)), ((), ())), preferred_element_type=F32)


def nn(a, b, precision=None):
    return jnp.dot(a, b, precision=precision, preferred_element_type=F32)


def farthest_first(j):
    return GRP // 2 + (j + 1) // 2 * (2 * (j % 2) - 1)


def iota(shape, dim):
    return lax.broadcasted_iota(jnp.int32, shape, dim)


def kernel(
    child, parent, cp_row, own_row, gate, ngain, wq, wk, wv, hgain, wo, fgain, wu, wd,
    out,
    child_q, parent_q, child_v, parent_v, wqkv, wo_v, wu_v, wd_v,
    joined, pick_t, outgoing, slots, normed, qkv, att, ccol, crow, loc, offs,
    s_send, s_recv, p_send, p_recv, t_send, t_recv, heads_out, back,
    part, via, comb, fin, hid, hb,
    in_sem, a_send, a_recv, g_send, g_recv, st_send, st_recv, pf_send, pf_recv, b_send, b_recv,
    v_send, v_recv, f_send, f_recv, h_send, h_recv, w_send, w_recv, t_sent, t_got,
):
    me = lax.axis_index("seq")
    fx = lax.axis_index("ffn")
    my_y = me // GRP
    my_zc = me % GRP
    left, right, far = (fx + 3) % 4, (fx + 1) % 4, (fx + 2) % 4

    cols = pl.ds(pl.multiple_of(fx * Q, Q), Q)
    loads = [
        (child.at[:, cols], child_q),
        (parent.at[:, cols], parent_q),
        (child, child_v),
        (parent, parent_v),
        (wq, wqkv.at[:, pl.ds(0, Q)]),
        (wk, wqkv.at[:, pl.ds(Q, Q)]),
        (wv, wqkv.at[:, pl.ds(2 * Q, Q)]),
        (wo, wo_v.at[fx]),
        (wu, wu_v),
        (wd, wd_v),
    ]
    loads = [pltpu.make_async_copy(s, d, in_sem.at[i]) for i, (s, d) in enumerate(loads)]
    for copy in loads[:2]:
        copy.start()

    barrier = pltpu.get_barrier_semaphore()

    def greet(k, _):
        pl.semaphore_signal(
            barrier, inc=1, device_id=((me + k) % N, fx), device_id_type=MESH
        )
        return 0

    lax.fori_loop(1, N, greet, 0)
    for k in (1, 2, 3):
        pl.semaphore_signal(barrier, inc=1, device_id=(me, (fx + k) % 4), device_id_type=MESH)

    owners = own_row[...]
    matched = (iota((N, TOK), 0) == owners).astype(F32)
    upper = (iota((TOK, TOK), 0) <= iota((TOK, TOK), 1)).astype(F32).astype(BF16)
    counts = nn(matched.astype(BF16), upper)
    within = jnp.sum(matched * (counts - 1.0), axis=0, keepdims=True)
    target = owners.astype(F32) * float(CAP) + within
    target_int = (target + 0.5).astype(jnp.int32)
    parents = (iota((PAR, TOK), 0) == cp_row[...]).astype(F32).astype(BF16)
    loads[0].wait()
    loads[1].wait()
    for copy in loads[2:]:
        copy.start()
    quarter = (child_q[...].astype(F32) + tn(parents, parent_q[...])).astype(BF16)

    def slot_copy(dest, rel):
        return pltpu.make_async_remote_copy(
            src_ref=outgoing.at[dest],
            dst_ref=slots.at[fx, me],
            send_sem=a_send,
            recv_sem=a_recv.at[(4 - rel) % 4],
            device_id=(dest, fx),
            device_id_type=MESH,
        )

    def place_group(rel):
        y = (my_y + rel) % 4
        pick = (iota((CH, TOK), 0) + y * CH == target_int).astype(F32).astype(BF16)
        outgoing[pl.ds(y * GRP, GRP)] = nn(pick, quarter).astype(BF16).reshape(GRP, CAP, Q)

    def send_group(rel):
        base = (my_y + rel) % 4 * GRP
        if rel == 0:
            pltpu.make_async_copy(outgoing.at[me], slots.at[fx, me], a_recv.at[0]).start()

        def send(j, _):
            slot_copy(base + (my_zc + farthest_first(j)) % GRP, rel).start()
            return 0

        lax.fori_loop(0, GRP - 1 if rel == 0 else GRP, send, 0)

    place_group(REL[0])
    pl.semaphore_wait(barrier, N - 1 + 3)
    send_group(REL[0])
    for rel in REL[1:]:
        place_group(rel)
        if REL.index(rel) < AHEAD:
            send_group(rel)

    eye = (iota((TOK, TOK), 0) == iota((TOK, TOK), 1)).astype(F32)
    target_col = nt(eye, jnp.broadcast_to(target, (8, TOK)), EXACT)[:, 0:1]
    pick_t[...] = (
        (iota((TOK, SLOT), 1) == (target_col + 0.5).astype(jnp.int32)).astype(F32).astype(BF16)
    )
    loads[2].wait()
    loads[3].wait()
    joined[...] = (child_v[...].astype(F32) + tn(parents, parent_v[...])).astype(BF16)

    causal = iota((CH, CH), 0) >= iota((CH, CH), 1)
    tri = causal.astype(F32)
    lane_head = iota((1, Q), 1) // HD

    def spread(columns):
        wide = jnp.zeros((columns.shape[0], Q), F32)
        for h in range(HEADS):
            wide = jnp.where(lane_head == h, columns[:, h : h + 1], wide)
        return wide

    block_end = jnp.zeros((1, HEADS), F32)
    for y in range(4):
        g = gate[:, pl.ds(y * CH, CH)]
        crow[y] = nt(g, tri, EXACT)
        columns = nt(tri, g, EXACT)
        ccol[y] = columns
        offs[y] = spread(block_end)
        block_end = block_end + columns[CH - 1 : CH, :]

    def ring(src, dst, send_sem, recv_sem, to):
        return pltpu.make_async_remote_copy(
            src_ref=src, dst_ref=dst, send_sem=send_sem, recv_sem=recv_sem,
            device_id=(me, to), device_id_type=MESH,
        )

    def gather_first(rel):
        rows = pl.ds((my_y + rel) % 4 * GRP, GRP)
        mine = slots.at[fx, rows]
        return [
            ring(mine, mine, g_send.at[rel, 0], g_recv.at[rel, 0], right),
            ring(mine, mine, g_send.at[rel, 1], g_recv.at[rel, 1], left),
        ]

    def gather_second(rel):
        start = (my_y + rel) % 4 * GRP
        a = slots.at[left, pl.ds(start, GRP // 2)]
        b = slots.at[right, pl.ds(start + GRP // 2, GRP // 2)]
        return [
            ring(a, a, g_send.at[rel, 2], g_recv.at[rel, 2], right),
            ring(b, b, g_send.at[rel, 3], g_recv.at[rel, 3], left),
        ]

    def slots_in(rel):
        here = slots.at[fx, pl.ds((my_y + rel) % 4 * GRP, GRP)]
        pltpu.make_async_copy(here, here, a_recv.at[rel]).wait()
        for copy in gather_first(rel):
            copy.start()
        place = REL.index((4 - rel) % 4) + AHEAD
        if place < 4:
            send_group(REL[place])

    def slots_on(rel):
        for copy, after in zip(gather_first(rel), gather_second(rel)):
            copy.wait_recv()
            after.start()

    def project(rel):
        y = (my_y + rel) % 4
        for copy in gather_second(rel):
            copy.wait_recv()
        squares = jnp.zeros((CH, 1), F32)
        for q in range(4):
            x = slots[q, pl.ds(y * GRP, GRP)].reshape(CH, Q).astype(F32)
            squares = squares + jnp.sum(x * x, axis=1, keepdims=True)
        scale = lax.rsqrt(squares / D + EPS)
        for q in range(4):
            x = slots[q, pl.ds(y * GRP, GRP)].reshape(CH, Q).astype(F32)
            gain = ngain[pl.ds(q * Q, Q)].astype(F32).reshape(1, Q)
            normed[:, pl.ds(q * Q, Q)] = (x * scale * gain).astype(BF16)
        qkv[y] = nn(normed[...], wqkv[...]).astype(BF16)

    order = [(4 - rel) % 4 for rel in REL]
    for i in range(6):
        if i < 4:
            slots_in(order[i])
        if 1 <= i < 5:
            slots_on(order[i - 1])
        if i == 1:
            for copy in loads[4:7]:
                copy.wait()
        if i >= 2:
            project(order[i - 2])

    def weights_first():
        mine = wo_v.at[fx]
        return [
            ring(mine, mine, w_send.at[0], w_recv.at[0], right),
            ring(mine, mine, w_send.at[1], w_recv.at[1], left),
        ]

    def weights_second():
        a, b = wo_v.at[left, pl.ds(0, Q // 2)], wo_v.at[right, pl.ds(Q // 2, Q // 2)]
        return [
            ring(a, a, w_send.at[2], w_recv.at[2], right),
            ring(b, b, w_send.at[3], w_recv.at[3], left),
        ]

    loads[7].wait()
    for copy in weights_first():
        copy.start()

    same_head = iota((Q, Q), 0) // HD == iota((Q, Q), 1) // HD
    carried = jnp.zeros((Q, Q), F32)
    for y in range(4):
        loc[y] = carried
        ends = ccol[y, pl.ds(CH - 1, 1), :]
        fade = jnp.exp(spread(ends - ccol[y]))
        added = tn(
            (qkv[y, :, pl.ds(Q, Q)].astype(F32) * fade).astype(BF16),
            qkv[y, :, pl.ds(2 * Q, Q)],
        )
        carried = jnp.exp(spread(ends)) * carried + jnp.where(same_head, added, 0.0)
    state = jnp.zeros((HD, Q), F32)
    for h in range(HEADS):
        state = state + carried[h * HD : (h + 1) * HD, :]
    lane = iota((1, 128), 1)
    ends = jnp.zeros((1, 128), F32)
    for h in range(HEADS):
        ends = jnp.where(lane == h, block_end[:, h : h + 1], ends)
    message = jnp.concatenate([state, jnp.broadcast_to(ends, (HD, 128))], axis=1)
    for r in range(4):
        s_send[:, r, :] = message[r * GRP : (r + 1) * GRP, :]

    def to_row(src, dst, send_sem, recv_sem):
        pltpu.make_async_copy(src.at[my_zc], dst.at[my_zc], recv_sem).start()

        def send(k, _):
            peer = (my_zc + farthest_first(k)) % GRP
            pltpu.make_async_remote_copy(
                src_ref=src.at[peer], dst_ref=dst.at[my_zc], send_sem=send_sem, recv_sem=recv_sem,
                device_id=(my_y * GRP + peer, fx), device_id_type=MESH,
            ).start()
            return 0

        lax.fori_loop(0, GRP - 1, send, 0)

    def totals_to(k):
        return pltpu.make_async_remote_copy(
            src_ref=t_send, dst_ref=t_recv.at[my_y],
            send_sem=t_sent.at[k - 1], recv_sem=t_got.at[k - 1],
            device_id=((my_y + k) % 4 * GRP + my_zc, fx), device_id_type=MESH,
        )

    def arrived(ref, sem):
        pltpu.make_async_copy(ref, ref, sem).wait()

    to_row(s_send, s_recv, st_send, st_recv)

    def inside(y):
        q = qkv[y, :, pl.ds(0, Q)]
        k = qkv[y, :, pl.ds(Q, Q)]
        v = qkv[y, :, pl.ds(2 * Q, Q)]
        total = jnp.zeros((CH, Q), F32)
        for h in range(HEADS):
            mine = (lane_head == h).astype(F32).astype(BF16)
            scores = nt(q * mine, k)
            spacing = ccol[y, :, pl.ds(h, 1)] - crow[y, pl.ds(h, 1), :]
            decay = jnp.where(causal, jnp.exp(jnp.minimum(spacing, 0.0)), 0.0)
            total = total + nn((scores * decay).astype(BF16), v * mine)
        att[y] = total

    inside(0)
    arrived(s_recv, st_recv)
    rows_got = [s_recv[:, r, :] for r in range(4)]
    got_ends = rows_got[0][:, Q:]
    states = jnp.concatenate([row[:, :Q] for row in rows_got], axis=1)
    tri_row = (iota((GRP, GRP), 0) >= iota((GRP, GRP), 1)).astype(F32)
    upto = nn(tri_row, got_ends, EXACT)
    row_end = upto[GRP - 1 :, :]
    before = jnp.concatenate([upto - got_ends, jnp.broadcast_to(row_end, (8, 128))], axis=0)
    upto_t = upto.T
    earlier = iota((GRP + 8, GRP), 0) > iota((GRP + 8, GRP), 1)
    wide_head = iota((1, 4 * Q), 1) // HD % HEADS
    prefix = jnp.zeros((GRP + 8, 4 * Q), F32)
    passing = jnp.zeros((GRP, 4 * Q), F32)
    for h in range(HEADS):
        spacing = before[:, h : h + 1] - upto_t[h : h + 1, :]
        weight = jnp.where(earlier, jnp.exp(jnp.minimum(spacing, 0.0)), 0.0)
        prefix = jnp.where(wide_head == h, nn(weight, states, EXACT), prefix)
        passing = jnp.where(wide_head == h, jnp.exp(before[:GRP, h : h + 1]), passing)
    t_send[...] = jnp.concatenate([prefix[GRP : GRP + 1, :], row_end], axis=1)
    for k in (2, 1, 3):
        totals_to(k).start()
    t_recv[my_y] = t_send[...]
    inside(1)
    for k in (1, 2, 3):
        totals_to(k).wait_recv()
    row_in = jnp.zeros((1, 4 * Q), F32)
    for y in range(3):
        total = t_recv[y]
        fading = jnp.zeros((1, 4 * Q), F32)
        for h in range(HEADS):
            fading = jnp.where(
                wide_head == h, jnp.exp(total[:, 4 * Q + h : 4 * Q + h + 1]), fading
            )
        row_in = jnp.where(y < my_y, fading * row_in + total[:, : 4 * Q], row_in)
    prefix = prefix[:GRP, :] + passing * row_in
    for r in range(4):
        p_send[:, r, :] = prefix[:, r * Q : (r + 1) * Q]
    to_row(p_send, p_recv, pf_send, pf_recv)
    inside(2)
    inside(3)
    arrived(p_recv, pf_recv)
    for copy, after in zip(weights_first(), weights_second()):
        copy.wait_recv()
        after.start()
    incoming = jnp.concatenate([p_recv[:, r, :] for r in range(4)], axis=0)
    incoming = jnp.where(same_head, jnp.concatenate([incoming] * HEADS, axis=0), 0.0)

    ones_head = same_head.astype(F32).astype(BF16)
    for rel in REL:
        y = (my_y + rel) % 4
        at_start = jnp.exp(offs[y]) * incoming + loc[y]
        outside = nn(qkv[y, :, pl.ds(0, Q)], at_start.astype(BF16))
        o = att[y] + jnp.exp(spread(ccol[y])) * outside
        squares = o * o
        high = squares.astype(BF16)
        low = (squares - high.astype(F32)).astype(BF16)
        mean = (nn(high, ones_head) + nn(low, ones_head)) / HD
        o = o * lax.rsqrt(mean + EPS) * hgain[...].astype(F32).reshape(1, Q)
        heads_out[pl.ds(y * GRP, GRP)] = o.astype(BF16).reshape(GRP, CAP, Q)
        if rel == 0:
            pltpu.make_async_copy(heads_out.at[me], back.at[me], b_recv).start()

        def send(j, _, y=y):
            dest = y * GRP + (my_zc + farthest_first(j)) % GRP
            pltpu.make_async_remote_copy(
                src_ref=heads_out.at[dest], dst_ref=back.at[me], send_sem=b_send, recv_sem=b_recv,
                device_id=(dest, fx), device_id_type=MESH,
            ).start()
            return 0

        lax.fori_loop(0, GRP - 1 if rel == 0 else GRP, send, 0)

    top, bottom = pl.ds(0, HALF), pl.ds(HALF, HALF)

    def scatter_first(c):
        if c in SCATTER_DIRECT:
            return [
                ring(part.at[c, far, top], via.at[c, 0], v_send.at[c, 0], v_recv.at[c, 0], far),
                ring(part.at[c, far, bottom], via.at[c, 1], v_send.at[c, 1], v_recv.at[c, 1], far),
            ]
        return [
            ring(part.at[c, far, top], via.at[c, 0], v_send.at[c, 0], v_recv.at[c, 0], right),
            ring(part.at[c, far, bottom], via.at[c, 1], v_send.at[c, 1], v_recv.at[c, 1], left),
        ]

    def scatter_own(c):
        return [
            ring(part.at[c, right, bottom], fin.at[c, 0, 1], f_send.at[c, 0, 1], f_recv.at[c, 0, 1], right),
            ring(part.at[c, left, top], fin.at[c, 1, 0], f_send.at[c, 1, 0], f_recv.at[c, 1, 0], left),
        ]

    def scatter_joint(c):
        if c in SCATTER_DIRECT:
            return [
                ring(part.at[c, right, top], fin.at[c, 0, 0], f_send.at[c, 0, 0], f_recv.at[c, 0, 0], right),
                ring(part.at[c, left, bottom], fin.at[c, 1, 1], f_send.at[c, 1, 1], f_recv.at[c, 1, 1], left),
            ]
        return [
            ring(comb.at[c, 0], fin.at[c, 0, 0], f_send.at[c, 0, 0], f_recv.at[c, 0, 0], right),
            ring(comb.at[c, 1], fin.at[c, 1, 1], f_send.at[c, 1, 1], f_recv.at[c, 1, 1], left),
        ]

    def scatter_start(c, product):
        for q in range(4):
            part[c, q] = product[:, q * Q : (q + 1) * Q].astype(BF16)
        for copy in scatter_first(c) + scatter_own(c):
            copy.start()
        if c in SCATTER_DIRECT:
            for copy in scatter_joint(c):
                copy.start()

    def scatter_on(c):
        if c in SCATTER_DIRECT:
            return
        pieces = [(right, top), (left, bottom)]
        for d, (copy, after) in enumerate(zip(scatter_first(c), scatter_joint(c))):
            copy.wait_recv()
            whose, rows = pieces[d]
            comb[c, d] = (
                part[c, whose, rows, :].astype(F32) + via[c, d].astype(F32)
            ).astype(BF16)
            after.start()

    def scattered(c):
        for copy in scatter_own(c) + scatter_joint(c):
            copy.wait_recv()
        total = part[c, fx].astype(F32)
        if c in SCATTER_DIRECT:
            for copy in scatter_first(c):
                copy.wait_recv()
            total = total + via[c].reshape(ROWS, Q).astype(F32)
        for d in range(2):
            total = total + fin[c, d].reshape(ROWS, Q).astype(F32)
        return total

    def hidden_first(c):
        mine = hb.at[fx, c]
        return [
            ring(mine, mine, h_send.at[c, 0], h_recv.at[c, 0], right),
            ring(mine, mine, h_send.at[c, 1], h_recv.at[c, 1], left),
        ]

    def hidden_second(c):
        if c in GATHER_DIRECT:
            mine = hb.at[fx, c]
            return [ring(mine, mine, h_send.at[c, 2], h_recv.at[c, 2], far)]
        a, b = hb.at[left, c, top], hb.at[right, c, bottom]
        return [
            ring(a, a, h_send.at[c, 2], h_recv.at[c, 2], right),
            ring(b, b, h_send.at[c, 3], h_recv.at[c, 3], left),
        ]

    def hidden_on(c):
        if c in GATHER_DIRECT:
            for copy in hidden_first(c):
                copy.wait_recv()
            return
        for copy, after in zip(hidden_first(c), hidden_second(c)):
            copy.wait_recv()
            after.start()

    def feed_forward(c):
        rows = pl.ds(c * ROWS, ROWS)
        for copy in hidden_second(c):
            copy.wait_recv()
        heads = jnp.concatenate([hb[q, c] for q in range(4)], axis=1)
        hidden = joined[rows, :].astype(F32) + nn(heads, wo_v[...].reshape(D, D))
        for q in range(4):
            hid[c, q] = hidden[:, q * Q : (q + 1) * Q]
        scale = lax.rsqrt(jnp.sum(hidden * hidden, axis=1, keepdims=True) / D + EPS)
        second = (hidden * scale * fgain[...].astype(F32).reshape(1, D)).astype(BF16)
        expanded = jax.nn.gelu(nn(second, wu_v[...])).astype(BF16)
        scatter_start(c, nn(expanded, wd_v[...]))

    def finish(c):
        out[pl.ds(c * ROWS, ROWS), :] = (hid[c, fx] + scattered(c)).astype(BF16)

    arrived(back, b_recv)
    for c in range(PARTS):
        rows = pl.ds(c * ROWS, ROWS)
        hb[fx, c] = nn(pick_t[rows, :], back[...].reshape(SLOT, Q)).astype(BF16)
        for copy in hidden_first(c) + (hidden_second(c) if c in GATHER_DIRECT else []):
            copy.start()
    for copy in loads[8:]:
        copy.wait()
    for copy in weights_second():
        copy.wait_recv()
    steps = [(0, hidden_on), (1, feed_forward), (2, scatter_on), (3, finish)]
    for i in range(PARTS + 4):
        for delay, step in steps:
            if 0 <= i - delay < PARTS:
                step(i - delay)

    arrived(outgoing.at[pl.ds(0, N - 1)], a_send)
    arrived(s_send.at[pl.ds(0, GRP - 1)], st_send)
    arrived(p_send.at[pl.ds(0, GRP - 1)], pf_send)
    for k in (1, 2, 3):
        totals_to(k).wait_send()
    arrived(heads_out.at[pl.ds(0, N - 1)], b_send)
    for rel in range(4):
        for copy in gather_first(rel) + gather_second(rel):
            copy.wait_send()
    for c in range(PARTS):
        for copy in hidden_first(c) + hidden_second(c):
            copy.wait_send()
        for copy in scatter_first(c) + scatter_own(c) + scatter_joint(c):
            copy.wait_send()
    for copy in weights_first() + weights_second():
        copy.wait_send()


def on_device(
    child_feat, parent_feat, child_parent, owner, log_gate, norm_gain, w_query, w_key, w_value,
    head_gain, w_out, ffn_gain, w_up, w_down,
):
    vmem = pl.BlockSpec(memory_space=pltpu.VMEM)
    anywhere = pl.BlockSpec(memory_space=pl.ANY)
    dma = pltpu.SemaphoreType.DMA
    return pl.pallas_call(
        kernel,
        out_shape=jax.ShapeDtypeStruct((TOK, Q), BF16),
        in_specs=[
            anywhere, anywhere, vmem, vmem, vmem, vmem, anywhere, anywhere, anywhere, vmem,
            anywhere, vmem, anywhere, anywhere,
        ],
        out_specs=vmem,
        scratch_shapes=[
            pltpu.VMEM((TOK, Q), BF16),
            pltpu.VMEM((PAR, Q), BF16),
            pltpu.VMEM((TOK, D), BF16),
            pltpu.VMEM((PAR, D), BF16),
            pltpu.VMEM((D, 3 * Q), BF16),
            pltpu.VMEM((4, Q, D), BF16),
            pltpu.VMEM((D, D), BF16),
            pltpu.VMEM((D, D), BF16),
            pltpu.VMEM((TOK, D), BF16),
            pltpu.VMEM((TOK, SLOT), BF16),
            pltpu.VMEM((N, CAP, Q), BF16),
            pltpu.VMEM((4, N, CAP, Q), BF16),
            pltpu.VMEM((CH, D), BF16),
            pltpu.VMEM((4, CH, 3 * Q), BF16),
            pltpu.VMEM((4, CH, Q), F32),
            pltpu.VMEM((4, CH, HEADS), F32),
            pltpu.VMEM((4, HEADS, CH), F32),
            pltpu.VMEM((4, Q, Q), F32),
            pltpu.VMEM((4, 1, Q), F32),
            pltpu.VMEM((GRP, 4, Q + 128), F32),
            pltpu.VMEM((GRP, 4, Q + 128), F32),
            pltpu.VMEM((GRP, 4, Q), F32),
            pltpu.VMEM((GRP, 4, Q), F32),
            pltpu.VMEM((1, 4 * Q + 128), F32),
            pltpu.VMEM((4, 1, 4 * Q + 128), F32),
            pltpu.VMEM((N, CAP, Q), BF16),
            pltpu.VMEM((N, CAP, Q), BF16),
            pltpu.VMEM((PARTS, 4, ROWS, Q), BF16),
            pltpu.VMEM((PARTS, 2, HALF, Q), BF16),
            pltpu.VMEM((PARTS, 2, HALF, Q), BF16),
            pltpu.VMEM((PARTS, 2, 2, HALF, Q), BF16),
            pltpu.VMEM((PARTS, 4, ROWS, Q), F32),
            pltpu.VMEM((4, PARTS, ROWS, Q), BF16),
            dma((10,)),
            dma,
            dma((4,)),
            dma((4, 4)),
            dma((4, 4)),
            dma, dma, dma, dma, dma, dma,
            dma((PARTS, 2)),
            dma((PARTS, 2)),
            dma((PARTS, 2, 2)),
            dma((PARTS, 2, 2)),
            dma((PARTS, 4)),
            dma((PARTS, 4)),
            dma((4,)),
            dma((4,)),
            dma((3,)),
            dma((3,)),
        ],
        compiler_params=pltpu.CompilerParams(
            collective_id=0, has_side_effects=True, vmem_limit_bytes=56 * 1024 * 1024
        ),
        name="block",
    )(
        child_feat,
        parent_feat,
        child_parent.reshape(1, TOK),
        owner.reshape(1, TOK),
        log_gate,
        norm_gain,
        w_query,
        w_key,
        w_value,
        head_gain,
        w_out,
        ffn_gain,
        w_up,
        w_down,
    )


def solution(mesh):
    seq, ffn = "seq", "ffn"
    in_specs = (
        P(seq, None), P(seq, None), P(seq), P(seq, None), P(ffn, seq), P(), P(None, ffn),
        P(None, ffn), P(None, ffn), P(ffn), P(ffn, None), P(), P(None, ffn), P(ffn, None),
    )
    return jax.shard_map(
        on_device, mesh=mesh, in_specs=in_specs, out_specs=P(seq, ffn), check_vma=False
    )
```
